32 devices in a mesh: grp: 4 (over z), shard: 8 (over y, x, core).
Axes of the slice: x: 2, y: 2, z: 4, core: 2. Of those that a mesh axis runs over, the one named last changes fastest.
Arguments:
- table: float32 [1024, 8, 128], P('shard')
- table_first: float32 [1024, 8, 128], P('shard'), may hold values from -3 to 3
- table_second: float32 [1024, 8, 128], P('shard')
- slot_table: int32 [1024], P('shard'), may hold values from 0 to 25
- touched: int32 [4, 256], P('grp', 'shard'), may hold values from 0 to 1023, as said below
- emb_grads: bfloat16 [4, 256, 8, 128], P('grp', 'shard'), may hold values from -6 to 6
- block_slot: int32 [1024], replicated, may hold values from 0 to 1023, as said below
- dense_x: bfloat16 [13, 131072], P(None, ('grp', 'shard')), may hold values from -6 to 6
- dense_cot: bfloat16 [131072, 128], P(('grp', 'shard')), may hold values from -0.15625 to 0.15625
- w_one: float32 [13, 512], replicated, may hold values from -1.75 to 1.75
- w_two: float32 [512, 256], replicated, may hold values from -0.25 to 0.25
- w_three: float32 [256, 128], replicated, may hold values from -0.375 to 0.375
- first_one: float32 [13, 512], replicated, may hold values from -3 to 3
- first_two: float32 [512, 256], replicated, may hold values from -3 to 3
- first_three: float32 [256, 128], replicated, may hold values from -3 to 3
- second_one: float32 [13, 512], replicated, may hold values from 0.001 to 0.3
- second_two: float32 [512, 256], replicated, may hold values from 0.001 to 0.3
- second_three: float32 [256, 128], replicated, may hold values from 0.001 to 0.3
Outputs:
- new_table: float32 [1024, 8, 128], P('shard')
- new_table_first: float32 [1024, 8, 128], P('shard')
- new_table_second: float32 [1024, 8, 128], P('shard')
- new_w_one: float32 [13, 512], replicated
- new_w_two: float32 [512, 256], replicated
- new_w_three: float32 [256, 128], replicated
- new_first_one: float32 [13, 512], replicated
- new_first_two: float32 [512, 256], replicated
- new_first_three: float32 [256, 128], replicated
- new_second_one: float32 [13, 512], replicated
- new_second_two: float32 [512, 256], replicated
- new_second_three: float32 [256, 128], replicated
The draws below stay inside these ranges and needn't reach their ends.
Inputs may be any that keep to these rules, and one draw needn't show every extreme that they name: `touched`: each device's 32 ids are distinct; at most 8 of them have block_slot // 128 equal to any one shard, and in every draw some shard gets exactly 8 from every device. `block_slot`: A permutation of the 1024 slots.
All inputs are finite; a program needn't handle non-finite values.
Results may differ from the reference program's by a relative error of at most 0.0037.
Values may be sent and summed in bfloat16 or wider, within the bound.
A program may use at most 128 MiB of HBM per device.

```python
import math
import jax
import jax.numpy as jnp
from jax import lax

E = 128
DIN = 13
H1 = 512
H2 = 256
TABLES = 26
BLK = 8
CAP = 8
NB_DEV = 128
TOK_DEV = 4096
K = 32
NB = 1024
TOKENS = 131072
N_GRP = 4
N_SHARD = 8


def common_slots(key):
    forward = jax.random.permutation(jax.random.fold_in(key, 11), NB).astype(jnp.int32)
    inverse = jnp.zeros((NB,), jnp.int32).at[forward].set(jnp.arange(NB, dtype=jnp.int32))
    return (forward, inverse)


def draw_block_slot(key, part):
    return common_slots(key)[0]


def draw_touched(key, part):
    forward, inverse = common_slots(key)
    devices_all = N_GRP * N_SHARD
    candidates = N_SHARD * CAP
    live_count = max(CAP, NB_DEV * 5 // 8)
    hottest = jax.random.randint(jax.random.fold_in(key, 12), (), 0, N_SHARD)
    owner_bias = jax.random.randint(jax.random.fold_in(key, 13), (devices_all, N_SHARD), 0, 4)
    owner_bias = jnp.where(jnp.arange(N_SHARD)[None, :] == hottest, 8, owner_bias)
    noise_keys = jax.random.split(jax.random.fold_in(key, 14), devices_all)
    noise = jax.vmap(lambda subkey: jax.random.permutation(subkey, candidates))(noise_keys).astype(jnp.int32)
    cand_owner = jnp.arange(candidates, dtype=jnp.int32) // CAP
    scores = owner_bias[:, cand_owner] * 1048576 + noise
    unused, chosen = lax.top_k(scores, K)
    owner_keys = jax.random.split(jax.random.fold_in(key, 17), N_SHARD)
    live_sets = jax.vmap(lambda subkey: jax.random.permutation(subkey, NB_DEV)[:live_count])(owner_keys).astype(jnp.int32)
    row_keys = jax.random.split(jax.random.fold_in(key, 15), devices_all * N_SHARD)
    live_pick = jax.vmap(lambda subkey: jax.random.permutation(subkey, live_count)[:CAP])(row_keys).astype(jnp.int32)
    live_pick = live_pick.reshape(devices_all, N_SHARD, CAP)
    owner_rows = jnp.arange(N_SHARD, dtype=jnp.int32)[None, :, None]
    local_rows = live_sets[owner_rows, live_pick].reshape(devices_all, candidates)
    local_pick = jnp.take_along_axis(local_rows, chosen, axis=1)
    slot_pick = chosen // CAP * NB_DEV + local_pick
    block_ids = inverse[slot_pick]
    order_keys = jax.random.split(jax.random.fold_in(key, 16), devices_all)
    orders = jax.vmap(lambda subkey: jax.random.permutation(subkey, K))(order_keys).astype(jnp.int32)
    block_ids = jnp.take_along_axis(block_ids, orders, axis=1)
    return block_ids.reshape(N_GRP, N_SHARD * K).astype(jnp.int32)


def slot_rise():
    slot_pos = jnp.arange(NB, dtype=jnp.float32)
    return 1.0 + 2.0 * slot_pos / max(NB - 1, 1)


def draw_table(key, part):
    rise = slot_rise()
    row_scale = 10.0 ** jax.random.uniform(jax.random.fold_in(key, 21), (NB, BLK, 1), jnp.float32)
    col_scale = 10.0 ** (jax.random.uniform(jax.random.fold_in(key, 22), (1, 1, E), jnp.float32) - 1.0)
    base = jax.random.normal(jax.random.fold_in(key, 23), (NB, BLK, E), jnp.float32)
    return (base * row_scale * col_scale * rise[:, None, None]).astype(jnp.float32)


def draw_table_second(key, part):
    rise = slot_rise()
    expo = jax.random.uniform(jax.random.fold_in(key, 31), (NB, BLK, E), jnp.float32, -3.0, -0.5)
    return (10.0 ** expo / (rise * rise)[:, None, None]).astype(jnp.float32)


def place_ends(drawn, rng, smallest, largest):
    dims = drawn.shape
    place = [jax.random.randint(jax.random.fold_in(rng, axis), (), 0, dims[axis]) for axis in range(len(dims))]
    drawn = drawn.at[tuple(place)].set(smallest)
    longest = dims.index(max(dims))
    place[longest] = (place[longest] + 1) % dims[longest]
    return drawn.at[tuple(place)].set(largest)


def levels(key, shape, cuts, low, top_value):
    loudness = 1.0
    for position, blocks in cuts:
        heights = jax.random.uniform(jax.random.fold_in(jax.random.fold_in(key, 6), position), (blocks,), jnp.float32, low / len(cuts), top_value / len(cuts))
        loudness = loudness * jnp.repeat(jnp.exp(heights), shape[position] // blocks).reshape((-1,) + (1,) * (len(shape) - 1 - position))
    return loudness


def gaussian(own_key, extent, width, most, cuts=(), kind=jnp.bfloat16):
    gain = levels(own_key, extent, cuts, -0.22, 0.18) if cuts else 1.0
    entries = jax.random.normal(own_key, extent, jnp.float32) * width * gain
    return jnp.minimum(jnp.maximum(entries, -most), most).astype(kind)


def setup_inputs(seed: int = 0) -> dict:
    keys = jax.random.split(jax.random.key(seed), 19)
    return {
        "table": draw_table(jax.random.fold_in(keys[18], 71), 0),
        "table_first": gaussian(keys[1], (NB, BLK, E), 0.2, 3.0, ((0, 8),), jnp.float32),
        "table_second": draw_table_second(jax.random.fold_in(keys[18], 71), 0),
        "slot_table": place_ends(jax.random.randint(keys[3], (NB,), 0, TABLES), jax.random.fold_in(keys[3], 1), 0, TABLES - 1).astype(jnp.int32),
        "touched": draw_touched(jax.random.fold_in(keys[18], 71), 0),
        "emb_grads": gaussian(keys[5], (N_GRP, N_SHARD * K, BLK, E), 1.0, 6.0, ((0, 4), (1, 8))),
        "block_slot": draw_block_slot(jax.random.fold_in(keys[18], 71), 0),
        "dense_x": gaussian(keys[7], (DIN, TOKENS), 1.0, 6.0, ((1, 32),)),
        "dense_cot": gaussian(keys[8], (TOKENS, E), (4 * TOKENS ** -0.5), 0.15625, ((0, 32),)),
        "w_one": gaussian(keys[9], (DIN, H1), DIN ** -0.5, 1.75, (), jnp.float32),
        "w_two": gaussian(keys[10], (H1, H2), H1 ** -0.5, 0.25, (), jnp.float32),
        "w_three": gaussian(keys[11], (H2, E), H2 ** -0.5, 0.375, (), jnp.float32),
        "first_one": gaussian(keys[12], (DIN, H1), 0.2, 3.0, (), jnp.float32),
        "first_two": gaussian(keys[13], (H1, H2), 0.2, 3.0, (), jnp.float32),
        "first_three": gaussian(keys[14], (H2, E), 0.2, 3.0, (), jnp.float32),
        "second_one": jnp.clip(jnp.exp(jax.random.uniform(keys[15], (DIN, H1), jnp.float32, math.log(0.001), math.log(0.3))), 0.001, 0.3),
        "second_two": jnp.clip(jnp.exp(jax.random.uniform(keys[16], (H1, H2), jnp.float32, math.log(0.001), math.log(0.3))), 0.001, 0.3),
        "second_three": jnp.clip(jnp.exp(jax.random.uniform(keys[17], (H2, E), jnp.float32, math.log(0.001), math.log(0.3))), 0.001, 0.3),
    }


beta_one = 0.9
beta_two = 0.999
corr_first = 1.0 - 0.9 ** 10
corr_second = 1.0 - 0.999 ** 10
adam_eps = 1e-06
decay_rate = 0.01
learn_rate = 0.1
ratio_eps = 1e-06

def silu_slope(pre_value):
    logistic = jax.nn.sigmoid(pre_value)
    return logistic * (1.0 + pre_value * (1.0 - logistic))

def tower_grads(dense_x, dense_cot, w_one, w_two, w_three):
    w_one_bf = w_one.astype(jnp.bfloat16)
    w_two_bf = w_two.astype(jnp.bfloat16)
    w_three_bf = w_three.astype(jnp.bfloat16)
    pre_one = lax.dot_general(dense_x, w_one_bf, (((0,), (0,)), ((), ())), preferred_element_type=jnp.float32)
    hidden_one = jax.nn.silu(pre_one).astype(jnp.bfloat16)
    pre_two = jnp.dot(hidden_one, w_two_bf, preferred_element_type=jnp.float32)
    hidden_two = jax.nn.silu(pre_two).astype(jnp.bfloat16)
    grad_three = lax.dot_general(hidden_two, dense_cot, (((0,), (0,)), ((), ())), preferred_element_type=jnp.float32)
    back_two = (lax.dot_general(dense_cot, w_three_bf, (((1,), (1,)), ((), ())), preferred_element_type=jnp.float32) * silu_slope(pre_two)).astype(jnp.bfloat16)
    grad_two = lax.dot_general(hidden_one, back_two, (((0,), (0,)), ((), ())), preferred_element_type=jnp.float32)
    back_one = (lax.dot_general(back_two, w_two_bf, (((1,), (1,)), ((), ())), preferred_element_type=jnp.float32) * silu_slope(pre_one)).astype(jnp.bfloat16)
    grad_one = jnp.dot(dense_x, back_one, preferred_element_type=jnp.float32)
    return (grad_one, grad_two, grad_three)

def lamb_dense(weight, first_in, second_in, gradient):
    first_out = beta_one * first_in + (1.0 - beta_one) * gradient
    second_out = beta_two * second_in + (1.0 - beta_two) * gradient * gradient
    update = first_out / corr_first / (jnp.sqrt(second_out / corr_second) + adam_eps) + decay_rate * weight
    trust_ratio = jnp.sqrt(jnp.sum(weight * weight)) / (jnp.sqrt(jnp.sum(update * update)) + ratio_eps)
    return (weight - learn_rate * trust_ratio * update, first_out, second_out)

def reference(table, table_first, table_second, slot_table, touched, emb_grads, block_slot, dense_x, dense_cot, w_one, w_two, w_three, first_one, first_two, first_three, second_one, second_two, second_three):
    slot_index = block_slot[touched].reshape(-1)
    flat_grads = emb_grads.reshape(-1, BLK, E).astype(jnp.float32)
    emb_grad = jnp.zeros((NB, BLK, E), jnp.float32).at[slot_index].add(flat_grads)
    hits = jnp.zeros((NB,), jnp.float32).at[slot_index].add(jnp.ones(slot_index.shape, jnp.float32))
    touched_mask = (hits > 0.5)[:, None, None]
    new_first = jnp.where(touched_mask, beta_one * table_first + (1.0 - beta_one) * emb_grad, table_first)
    new_second = jnp.where(touched_mask, beta_two * table_second + (1.0 - beta_two) * emb_grad * emb_grad, table_second)
    update = jnp.where(touched_mask, new_first / corr_first / (jnp.sqrt(new_second / corr_second) + adam_eps) + decay_rate * table, 0.0)
    weight_sq = jax.ops.segment_sum(lax.optimization_barrier(jnp.sum(table * table, axis=(1, 2))), slot_table, TABLES)
    update_sq = jax.ops.segment_sum(lax.optimization_barrier(jnp.sum(update * update, axis=(1, 2))), slot_table, TABLES)
    table_ratio = jnp.sqrt(weight_sq) / (jnp.sqrt(update_sq) + ratio_eps)
    new_table = table - learn_rate * table_ratio[slot_table][:, None, None] * update
    blocks_all = N_GRP * N_SHARD
    x_blocks = dense_x.reshape(DIN, blocks_all, TOK_DEV).transpose(1, 0, 2)
    cot_blocks = dense_cot.reshape(blocks_all, TOK_DEV, E)

    def accumulate(totals, inputs):
        terms = tower_grads(inputs[0], inputs[1], w_one, w_two, w_three)
        return ((totals[0] + terms[0], totals[1] + terms[1], totals[2] + terms[2]), None)
    start_sums = (jnp.zeros((DIN, H1), jnp.float32), jnp.zeros((H1, H2), jnp.float32), jnp.zeros((H2, E), jnp.float32))
    grads, unused = lax.scan(accumulate, start_sums, (x_blocks, cot_blocks))
    layer_one = lamb_dense(w_one, first_one, second_one, grads[0])
    layer_two = lamb_dense(w_two, first_two, second_two, grads[1])
    layer_three = lamb_dense(w_three, first_three, second_three, grads[2])
    return (new_table, new_first, new_second, layer_one[0], layer_two[0], layer_three[0], layer_one[1], layer_two[1], layer_three[1], layer_one[2], layer_two[2], layer_three[2])
```

```python
import functools
import jax
import jax.numpy as jnp
from jax import lax
from jax.experimental import pallas as pl
from jax.experimental.pallas import tpu as pltpu
from jax.sharding import PartitionSpec as P

TABLES = 26
CAP = 8
HEAD = 2
TAIL = 1

beta_one = 0.9
beta_two = 0.999
corr_first = 1.0 - 0.9**10
corr_second = 1.0 - 0.999**10
adam_eps = 1e-06
decay_rate = 0.01
learn_rate = 0.1
ratio_eps = 1e-06

MESH = pl.DeviceIdType.MESH
F32 = jnp.float32
BF16 = jnp.bfloat16
NN = (((1,), (0,)), ((), ()))
NT = (((1,), (1,)), ((), ()))
TN = (((0,), (0,)), ((), ()))


def mm(a, b, dims=NN):
    return lax.dot_general(a, b, dims, preferred_element_type=F32)


def iota(shape, axis):
    return lax.broadcasted_iota(jnp.int32, shape, axis).astype(F32)


def to_col(row, eye):
    return jnp.sum(jnp.where(eye, row, 0.0), axis=1, keepdims=True)


def to_row(col, eye):
    return jnp.sum(jnp.where(eye, col, 0.0), axis=0, keepdims=True)


def square_eye(count):
    return iota((count, count), 0) == iota((count, count), 1)


def gate(pre):
    logistic = 0.5 * jnp.tanh(0.5 * pre) + 0.5
    hidden = pre * logistic
    return hidden, logistic + hidden * (1.0 - logistic)


def adam(first_in, second_in, gradient, weight):
    first_out = beta_one * first_in + (1.0 - beta_one) * gradient
    second_out = beta_two * second_in + (1.0 - beta_two) * gradient * gradient
    update = (
        first_out / corr_first / (jnp.sqrt(second_out / corr_second) + adam_eps)
        + decay_rate * weight
    )
    return first_out, second_out, update


def exchange_kernel(
    grps,
    shards,
    owners,
    chunk,
    touched_in,
    block_slot_in,
    slot_table_in,
    emb_in,
    x_in,
    cot_in,
    *refs,
):
    ins, refs = refs[:12], refs[12:]
    outs, refs = refs[:12], refs[12:]
    o_table, o_first, o_second = outs[:3]
    o_w, o_m, o_v = outs[3:6], outs[6:9], outs[9:12]
    (
        touched,
        block_slot,
        slot_table,
        emb_grads,
        x,
        cot,
        w1t,
        w2t,
        w2b,
        w3b,
        slope_buf,
        back_buf,
        acc_one,
        acc_two,
        acc_three,
        rows_f32,
        table_update,
        update_two,
        update_three,
        e_send,
        e_recv,
        t_send,
        t_recv,
        t_all,
        p_send,
        p_recv,
        q_send,
        r_recv,
        a_all,
        s_recv,
        y_plane,
        y_z,
        y_all,
        stats,
        plane_ssem,
        plane_rsem,
        z_ssem,
        z_rsem,
        core_ssem,
        core_rsem,
        chip_ssem,
        chip_rsem,
        load_sem,
    ) = refs
    g = lax.axis_index("grp")
    s = lax.axis_index("shard")
    c = lax.rem(s, 2)
    p = s // 2
    places = shards // 2
    chips = grps * places
    mine = g * places + p
    stride = chips // owners
    me = mine // stride
    width = emb_grads.shape[1]
    block_rows = 8
    count = touched.shape[1]
    slots = block_slot.shape[1]
    local_blocks = slot_table.shape[1]
    tokens = x.shape[1]
    din = x.shape[0]
    h_one, h_two = acc_two.shape
    out_dim = acc_three.shape[1]
    half_one, half_two = h_one // 2, h_two // 2
    fold_two = half_one // owners // 8
    fold_three = half_two // owners // 8

    barrier = pltpu.get_barrier_semaphore()

    def greet(device):
        pl.semaphore_signal(barrier, inc=1, device_id=device, device_id_type=MESH)

    for k in range(1, shards):
        greet((g, lax.rem(s + k, shards)))
    for kg in range(1, grps):
        for kp in range(places):
            greet((lax.rem(g + kg, grps), 2 * lax.rem(p + kp, places) + c))

    pairs = [
        (touched_in, touched),
        (block_slot_in, block_slot),
        (emb_in, emb_grads),
        (ins[3], o_w[0]),
        (ins[4], o_w[1]),
        (ins[5], o_w[2]),
        (x_in, x),
        (cot_in, cot),
        (slot_table_in, slot_table),
        (ins[0], o_table),
        (ins[1], o_first),
        (ins[2], o_second),
    ] + list(zip(ins[6:], outs[6:]))
    loads = [pltpu.make_async_copy(a, b, load_sem.at[i]) for i, (a, b) in enumerate(pairs)]
    for d in loads:
        d.start()

    def remote(src, dst, ssem, rsem, device):
        return pltpu.make_async_remote_copy(
            src_ref=src,
            dst_ref=dst,
            send_sem=ssem,
            recv_sem=rsem,
            device_id=device,
            device_id_type=MESH,
        )

    def plane(phase, k, src, dst):
        device = (g, lax.rem(s + k, shards))
        return remote(src, dst, plane_ssem.at[phase, k], plane_rsem.at[phase, k], device)

    def along(phase, k, src, dst):
        device = (lax.rem(g + k, grps), s)
        return remote(src, dst, z_ssem.at[phase, k], z_rsem.at[phase, k], device)

    def other(phase, src, dst):
        return remote(src, dst, core_ssem.at[phase], core_rsem.at[phase], (g, s + 1 - 2 * c))

    def chip(phase, src, dst, out_index, in_index, target):
        device = (target // places, 2 * lax.rem(target, places) + c)
        return remote(
            src, dst, chip_ssem.at[phase, out_index], chip_rsem.at[phase, in_index], device
        )

    sends = []

    def start(copies):
        for d in copies:
            d.start()
        sends.extend(copies)
        return copies

    def z_spread(phase, buf):
        return start([along(phase, k, buf.at[g], buf.at[g]) for k in range(1, grps)])

    def recv(copies):
        for d in copies:
            d.wait_recv()

    def owner_only(run):
        if stride == 1:
            run()
        else:
            pl.when(lax.rem(mine, stride) == 0)(run)

    def each_owner(run):
        for k in range(owners):
            i = lax.rem(me + k, owners)
            if k:
                run(i)
            elif stride > 1:
                pl.when(lax.rem(mine, stride) != 0)(functools.partial(run, i))

    def each_chip(run):
        for k in range(1, chips):
            run(lax.rem(mine + k, chips))

    def total(buf, n, *at):
        out = buf[(0,) + at].astype(F32)
        for i in range(1, n):
            out += buf[(i,) + at].astype(F32)
        return out

    for d in loads[:3]:
        d.wait()
    eye = square_eye(count)
    touched_col = to_col(touched[...].astype(F32), eye)
    hot = touched_col == iota((count, slots), 1)
    slot_col = jnp.sum(jnp.where(hot, block_slot[...].astype(F32), 0.0), axis=1, keepdims=True)
    slot_row = to_row(slot_col, eye)
    owner_col = jnp.floor((slot_col + 0.5) / local_blocks)
    owner_row = jnp.floor((slot_row + 0.5) / local_blocks)
    local_row = slot_row - owner_row * local_blocks
    earlier = (owner_col == owner_row) & (iota((count, count), 0) < iota((count, count), 1))
    rank_row = jnp.sum(jnp.where(earlier, 1.0, 0.0), axis=0, keepdims=True)
    send_row = owner_row * CAP + rank_row
    picker = iota((shards * CAP, count), 0) == send_row
    pick_f32 = jnp.where(picker, 1.0, 0.0)
    pick_bf = pick_f32.astype(BF16)
    filled = jnp.sum(pick_f32, axis=1, keepdims=True)
    local_col = jnp.sum(jnp.where(picker, local_row, 0.0), axis=1, keepdims=True)
    local_col = jnp.where(filled > 0.5, local_col, -1.0)
    rows_f32[...] = emb_grads[...].astype(F32)
    for r in range(block_rows):
        part = rows_f32[pl.ds(r, count, stride=block_rows), :].astype(BF16)
        picked = mm(pick_bf, part).reshape(shards, CAP, width)
        e_send[:, :, r * width : (r + 1) * width] = picked.astype(BF16)
    lanes = jnp.broadcast_to(local_col, (shards * CAP, width)).reshape(shards, CAP, width)
    t_send[...] = lanes.astype(BF16)
    e_recv[g, s] = e_send[s]
    t_recv[s] = t_send[s]

    pl.semaphore_wait(barrier, shards - 1 + (grps - 1) * places)
    e_plane = start(
        [plane(0, k, e_send.at[lax.rem(s + k, shards)], e_recv.at[g, s]) for k in range(1, shards)]
    )
    t_plane = start(
        [plane(1, k, t_send.at[lax.rem(s + k, shards)], t_recv.at[s]) for k in range(1, shards)]
    )

    for d in loads[3:8]:
        d.wait()
    w1t[...] = o_w[0][...].T.astype(BF16)
    w2t[...] = o_w[1][...].T.astype(BF16)
    w2b[...] = o_w[1][...].astype(BF16)
    w3b[...] = o_w[2][...].astype(BF16)
    acc_one[...] = jnp.zeros_like(acc_one)
    acc_two[...] = jnp.zeros_like(acc_two)
    acc_three[...] = jnp.zeros_like(acc_three)

    def forward(i, carry):
        tok = pl.ds(pl.multiple_of(i * chunk, chunk), chunk)
        hid, slope = gate(mm(w1t[...], x[:, tok]))
        hidden_one = hid.astype(BF16)
        slope_buf[:, tok] = slope
        hid, slope = gate(mm(w2t[...], hidden_one))
        cc = cot[tok, :]
        acc_three[...] += mm(hid.astype(BF16), cc)
        back = (mm(w3b[...], cc, NT) * slope).astype(BF16)
        back_buf[:, tok] = back
        acc_two[...] += mm(hidden_one, back, NT)
        return carry

    def backward(i, carry):
        tok = pl.ds(pl.multiple_of(i * chunk, chunk), chunk)
        back = (mm(w2b[...], back_buf[:, tok]) * slope_buf[:, tok]).astype(BF16)
        acc_one[0:din, :] += mm(x[:, tok], back, NT)
        return carry

    steps = tokens // chunk
    lead = min(HEAD, steps)
    lax.fori_loop(0, lead, forward, 0)
    recv(e_plane)
    e_z = z_spread(0, e_recv)
    recv(t_plane)
    group = shards * CAP
    tag_lanes = t_all.shape[2]
    tag_eye = iota((group, tag_lanes), 0) == iota((group, tag_lanes), 1)
    tag_row = to_row(t_recv[...].astype(F32).reshape(group, width)[:, 0:1], tag_eye)
    t_all[g] = jnp.broadcast_to(tag_row, t_all.shape[1:]).astype(BF16)
    t_z = z_spread(1, t_all)
    lax.fori_loop(lead, steps, forward, 0)

    base = fold_two * h_two

    def folded(part):
        two = acc_two[pl.ds(pl.multiple_of(part * half_one, half_one), half_one), :]
        three = acc_three[pl.ds(pl.multiple_of(part * half_two, half_two), half_two), :]
        two = two.reshape(owners, fold_two * 8, h_two)
        three = three.reshape(owners, fold_three * 8, out_dim)
        out = [(a * h_two, two[:, 8 * a : 8 * a + 8, :]) for a in range(fold_two)]
        return out + [
            (base + b * out_dim, three[:, 8 * b : 8 * b + 8, :]) for b in range(fold_three)
        ]

    for at, piece in folded(1 - c):
        p_send[:, :, at : at + piece.shape[2]] = piece.astype(BF16)
    c_p = start([other(0, p_send, p_recv)])
    late = max(0, steps - TAIL)
    lax.fori_loop(0, late, backward, 0)
    recv(c_p)
    for at, piece in folded(c):
        there = p_recv[:, :, at : at + piece.shape[2]].astype(F32)
        q_send[:, :, at : at + piece.shape[2]] = (piece + there).astype(BF16)

    def scatter(i):
        return chip(0, q_send.at[i], r_recv.at[mine], i, mine, i * stride)

    def gathered(m):
        return chip(0, q_send.at[0], r_recv.at[m], 0, m, m)

    def spread(m):
        return chip(1, a_all.at[c, me], a_all.at[c, me], m, me, m)

    def arrived(i):
        return chip(1, a_all.at[c, i], a_all.at[c, i], 0, i, i * stride)

    each_owner(lambda i: scatter(i).start())
    owner_only(lambda: r_recv.__setitem__(mine, q_send[me]))

    lax.fori_loop(late, steps, backward, 0)
    thin = acc_one.shape[0] // 2
    my_rows = pl.ds(pl.multiple_of(c * thin, thin), thin)
    its_rows = pl.ds(pl.multiple_of((1 - c) * thin, thin), thin)
    c_s = start([other(1, acc_one.at[its_rows], s_recv)])

    for d in loads[8:]:
        d.wait()
    slot_eye = square_eye(local_blocks)
    table_col = to_col(slot_table[...].astype(F32), slot_eye)
    table_hot = table_col == iota((local_blocks, 128), 1)
    row_weight = jnp.zeros((local_blocks, width), F32)
    for r in range(block_rows):
        weight = o_table[pl.ds(r, local_blocks, stride=block_rows), :]
        row_weight += weight * weight
    weight_col = jnp.sum(row_weight, axis=1, keepdims=True)
    weight_row = jnp.sum(jnp.where(table_hot, weight_col, 0.0), axis=0, keepdims=True)

    recv(c_s)
    y_plane[p] = (acc_one[my_rows, :] + s_recv[...]).astype(BF16)
    c_yp = []
    for k in range(1, places):
        device = (g, 2 * lax.rem(p + k, places) + c)
        c_yp.append(
            remote(y_plane.at[p], y_plane.at[p], plane_ssem.at[3, k], plane_rsem.at[3, k], device)
        )
    start(c_yp)

    def reduce_piece():
        each_chip(lambda m: gathered(m).wait_recv())
        a_all[c, me] = total(r_recv, chips).astype(BF16)
        each_chip(lambda m: spread(m).start())

    owner_only(reduce_piece)

    recv(c_yp)
    y_z[g] = total(y_plane, places).astype(BF16)
    c_yz = z_spread(2, y_z)

    slots_at = iota((local_blocks, group), 0)
    recv(t_z)
    matches = []
    for q in range(grps):
        tags = t_all[q, 0:1, 0:group].astype(F32)
        matches.append(jnp.where(slots_at == tags, 1.0, 0.0))
    hits = jnp.sum(sum(matches), axis=1, keepdims=True) > 0.5
    mask = jnp.broadcast_to(jnp.where(hits, 1.0, 0.0), (local_blocks, width)) > 0.5
    match_t = jnp.concatenate(matches, axis=1).astype(BF16)
    recv(e_z)
    row_update = jnp.zeros((local_blocks, width), F32)
    for r in range(block_rows):
        at = pl.ds(r, local_blocks, stride=block_rows)
        rows = e_recv[:, :, :, r * width : (r + 1) * width].astype(F32)
        summed = mm(match_t, rows.reshape(grps * group, width).astype(BF16))
        first_old, second_old = o_first[at, :], o_second[at, :]
        first, second, update = adam(first_old, second_old, summed, o_table[at, :])
        update = jnp.where(mask, update, 0.0)
        o_first[at, :] = jnp.where(mask, first, first_old)
        o_second[at, :] = jnp.where(mask, second, second_old)
        table_update[at, :] = update
        row_update += update * update
    update_col = jnp.sum(row_update, axis=1, keepdims=True)
    update_row = jnp.sum(jnp.where(table_hot, update_col, 0.0), axis=0, keepdims=True)
    stats[s] = jnp.concatenate([weight_row, update_row, jnp.zeros((6, 128), F32)], axis=0)
    c_st = start([plane(2, k, stats.at[s], stats.at[s]) for k in range(1, shards)])

    recv(c_yz)
    y_all[c] = total(y_z, grps)
    c_y = start([other(2, y_all.at[c], y_all.at[c])])
    weight_sq = [jnp.sum(w[...] * w[...], keepdims=True) for w in o_w]

    each_owner(lambda i: arrived(i).wait_recv())
    c_a = start([other(3, a_all.at[c], a_all.at[c])])

    def dense_step(j, rows, grad, keep):
        first, second, update = adam(o_m[j][rows, :], o_v[j][rows, :], grad, o_w[j][rows, :])
        o_m[j][rows, :] = first
        o_v[j][rows, :] = second
        if keep is not None:
            keep[rows, :] = update
        return update, jnp.sum(update * update, axis=0, keepdims=True)

    def half_step(part):
        two = [
            a_all[part, :, :, a * h_two : (a + 1) * h_two].astype(F32) for a in range(fold_two)
        ]
        three = [
            a_all[part, :, :, base + b * out_dim : base + (b + 1) * out_dim].astype(F32)
            for b in range(fold_three)
        ]
        two = jnp.concatenate(two, axis=1).reshape(half_one, h_two)
        three = jnp.concatenate(three, axis=1).reshape(half_two, out_dim)
        rows_two = pl.ds(pl.multiple_of(part * half_one, half_one), half_one)
        rows_three = pl.ds(pl.multiple_of(part * half_two, half_two), half_two)
        return (
            dense_step(1, rows_two, two, update_two)[1],
            dense_step(2, rows_three, three, update_three)[1],
        )

    def trust(j, update_sq):
        return (
            learn_rate
            * jnp.sqrt(weight_sq[j])
            / (jnp.sqrt(jnp.sum(update_sq, keepdims=True)) + ratio_eps)
        )

    here = half_step(c)
    recv(c_y)
    grad = y_all[...].reshape(2 * thin, h_one)[0:din, :]
    update, update_sq = dense_step(0, slice(None), grad, None)
    o_w[0][...] = o_w[0][...] - trust(0, update_sq) * update

    recv(c_st)
    tot = total(stats, shards)
    ratio = jnp.sqrt(tot[0:1]) / (jnp.sqrt(tot[1:2]) + ratio_eps)
    ratio_col = jnp.sum(jnp.where(table_hot, ratio, 0.0), axis=1, keepdims=True)
    rate = jnp.broadcast_to(learn_rate * ratio_col, (local_blocks, width))
    for r in range(block_rows):
        at = pl.ds(r, local_blocks, stride=block_rows)
        o_table[at, :] = o_table[at, :] - rate * table_update[at, :]

    recv(c_a)
    there = half_step(1 - c)
    o_w[1][...] = o_w[1][...] - trust(1, here[0] + there[0]) * update_two[...]
    o_w[2][...] = o_w[2][...] - trust(2, here[1] + there[1]) * update_three[...]

    for d in sends:
        d.wait_send()
    each_owner(lambda i: scatter(i).wait_send())
    owner_only(lambda: each_chip(lambda m: spread(m).wait_send()))


def store_kernel(*refs):
    srcs, outs, sem = refs[:12], refs[12:24], refs[24]
    stores = [pltpu.make_async_copy(a, b, sem.at[i]) for i, (a, b) in enumerate(zip(srcs, outs))]
    for d in stores:
        d.start()
    for d in stores:
        d.wait()


def body(
    table, table_first, table_second, slot_table, touched, emb_grads, block_slot,
    dense_x, dense_cot, *dense,
):
    shards = lax.axis_size("shard")
    grps = lax.axis_size("grp")
    blocks, block_rows, width = table.shape
    count = touched.shape[1]
    din, tokens = dense_x.shape
    h_one, h_two = dense[1].shape
    out_dim = dense[2].shape[1]
    chunk = min(1024, tokens)
    din_pad = -(-din // 16) * 16
    flat = (blocks * block_rows, width)
    e_width = block_rows * width
    tag_width = max(128, shards * CAP)
    places = shards // 2
    chips = grps * places
    owners = min(chips, h_one // 16, h_two // 16)
    fold = (h_one // (16 * owners)) * h_two + (h_two // (16 * owners)) * out_dim
    hbm = pl.BlockSpec(memory_space=pltpu.HBM)
    vmem = pl.BlockSpec(memory_space=pltpu.VMEM)
    sds = jax.ShapeDtypeStruct
    state = tuple(a.reshape(flat) for a in (table, table_first, table_second)) + dense
    shapes = tuple(sds(a.shape, F32) for a in state)
    held = pl.pallas_call(
        functools.partial(exchange_kernel, grps, shards, owners, chunk),
        out_shape=tuple(pltpu.VMEM(a.shape, F32) for a in state),
        in_specs=[hbm] * 18,
        out_specs=(vmem,) * 12,
        scratch_shapes=[
            pltpu.VMEM((1, count), jnp.int32),
            pltpu.VMEM((1, block_slot.shape[0]), jnp.int32),
            pltpu.VMEM((1, blocks), jnp.int32),
            pltpu.VMEM((count * block_rows, width), BF16),
            pltpu.VMEM(dense_x.shape, BF16),
            pltpu.VMEM(dense_cot.shape, BF16),
            pltpu.VMEM((h_one, din), BF16),
            pltpu.VMEM((h_two, h_one), BF16),
            pltpu.VMEM((h_one, h_two), BF16),
            pltpu.VMEM((h_two, out_dim), BF16),
            pltpu.VMEM((h_one, tokens), F32),
            pltpu.VMEM((h_two, tokens), BF16),
            pltpu.VMEM((din_pad, h_one), F32),
            pltpu.VMEM((h_one, h_two), F32),
            pltpu.VMEM((h_two, out_dim), F32),
            pltpu.VMEM((count * block_rows, width), F32),
            pltpu.VMEM(flat, F32),
            pltpu.VMEM((h_one, h_two), F32),
            pltpu.VMEM((h_two, out_dim), F32),
            pltpu.VMEM((shards, CAP, e_width), BF16),
            pltpu.VMEM((grps, shards, CAP, e_width), BF16),
            pltpu.VMEM((shards, CAP, width), BF16),
            pltpu.VMEM((shards, CAP, width), BF16),
            pltpu.VMEM((grps, 16, tag_width), BF16),
            pltpu.VMEM((owners, 8, fold), BF16),
            pltpu.VMEM((owners, 8, fold), BF16),
            pltpu.VMEM((owners, 8, fold), BF16),
            pltpu.VMEM((chips, 8, fold), BF16),
            pltpu.VMEM((2, owners, 8, fold), BF16),
            pltpu.VMEM((din_pad // 2, h_one), F32),
            pltpu.VMEM((places, din_pad // 2, h_one), BF16),
            pltpu.VMEM((grps, din_pad // 2, h_one), BF16),
            pltpu.VMEM((2, din_pad // 2, h_one), F32),
            pltpu.VMEM((shards, 8, 128), F32),
            pltpu.SemaphoreType.DMA((4, shards)),
            pltpu.SemaphoreType.DMA((4, shards)),
            pltpu.SemaphoreType.DMA((3, grps)),
            pltpu.SemaphoreType.DMA((3, grps)),
            pltpu.SemaphoreType.DMA((4,)),
            pltpu.SemaphoreType.DMA((4,)),
            pltpu.SemaphoreType.DMA((2, chips)),
            pltpu.SemaphoreType.DMA((2, chips)),
            pltpu.SemaphoreType.DMA((18,)),
        ],
        compiler_params=pltpu.CompilerParams(
            collective_id=0, has_side_effects=True, vmem_limit_bytes=40 << 20
        ),
        name="tower_exchange",
    )(
        *(
            pltpu.with_memory_space_constraint(a, pltpu.HBM)
            for a in (
                touched,
                block_slot.reshape(1, -1),
                slot_table.reshape(1, -1),
                emb_grads.reshape(count * block_rows, width),
                dense_x,
                dense_cot,
            )
            + state
        )
    )
    outs = pl.pallas_call(
        store_kernel,
        out_shape=shapes,
        in_specs=[vmem] * 12,
        out_specs=(pl.BlockSpec(memory_space=pl.ANY),) * 12,
        scratch_shapes=[pltpu.SemaphoreType.DMA((12,))],
        compiler_params=pltpu.CompilerParams(vmem_limit_bytes=12 << 20),
        name="store",
    )(*held)
    return tuple(o.reshape(table.shape) for o in outs[:3]) + tuple(outs[3:])


def solution(mesh):
    dense = (P(),) * 9
    rows = P("shard", None, None)
    return jax.shard_map(
        body,
        mesh=mesh,
        in_specs=(
            rows,
            rows,
            rows,
            P("shard"),
            P("grp", "shard"),
            P("grp", "shard", None, None),
            P(),
            P(None, ("grp", "shard")),
            P(("grp", "shard"), None),
        )
        + dense,
        out_specs=(rows,) * 3 + dense,
        check_vma=False,
    )
```

```python
import functools
import jax
import jax.numpy as jnp
from jax import lax
from jax.experimental import pallas as pl
from jax.experimental.pallas import tpu as pltpu
from jax.sharding import PartitionSpec as P

TABLES = 26
CAP = 8
HEAD = 2
TAIL = 2

beta_one = 0.9
beta_two = 0.999
corr_first = 1.0 - 0.9**10
corr_second = 1.0 - 0.999**10
adam_eps = 1e-06
decay_rate = 0.01
learn_rate = 0.1
ratio_eps = 1e-06

MESH = pl.DeviceIdType.MESH
F32 = jnp.float32
BF16 = jnp.bfloat16
NN = (((1,), (0,)), ((), ()))
NT = (((1,), (1,)), ((), ()))
TN = (((0,), (0,)), ((), ()))


def mm(a, b, dims=NN):
    return lax.dot_general(a, b, dims, preferred_element_type=F32)


def iota(shape, axis):
    return lax.broadcasted_iota(jnp.int32, shape, axis).astype(F32)


def to_col(row, eye):
    return jnp.sum(jnp.where(eye, row, 0.0), axis=1, keepdims=True)


def to_row(col, eye):
    return jnp.sum(jnp.where(eye, col, 0.0), axis=0, keepdims=True)


def square_eye(count):
    return iota((count, count), 0) == iota((count, count), 1)


def gate(pre):
    logistic = 0.5 * jnp.tanh(0.5 * pre) + 0.5
    hidden = pre * logistic
    return hidden, logistic + hidden * (1.0 - logistic)


def adam(first_in, second_in, gradient, weight):
    first_out = beta_one * first_in + (1.0 - beta_one) * gradient
    second_out = beta_two * second_in + (1.0 - beta_two) * gradient * gradient
    update = (
        first_out / corr_first / (jnp.sqrt(second_out / corr_second) + adam_eps)
        + decay_rate * weight
    )
    return first_out, second_out, update


def exchange_kernel(
    grps,
    shards,
    chunk,
    touched_in,
    block_slot_in,
    slot_table_in,
    emb_in,
    x_in,
    cot_in,
    *refs,
):
    ins, refs = refs[:12], refs[12:]
    outs, refs = refs[:12], refs[12:]
    o_table, o_first, o_second = outs[:3]
    o_w, o_m, o_v = outs[3:6], outs[6:9], outs[9:12]
    (
        touched,
        block_slot,
        slot_table,
        emb_grads,
        x,
        cot,
        w1t,
        w2t,
        w2b,
        w3b,
        slope_buf,
        hidden_buf,
        back_buf,
        acc_one,
        acc_two,
        acc_three,
        rows_f32,
        table_update,
        update_two,
        update_three,
        e_send,
        e_recv,
        t_send,
        t_recv,
        t_all,
        p_send,
        p_recv,
        q_send,
        r_recv,
        r_line,
        a_all,
        s_recv,
        y_plane,
        y_z,
        y_all,
        stats,
        plane_ssem,
        plane_rsem,
        z_ssem,
        z_rsem,
        core_ssem,
        core_rsem,
        load_sem,
    ) = refs
    g = lax.axis_index("grp")
    s = lax.axis_index("shard")
    c = lax.rem(s, 2)
    p = s // 2
    places = shards // 2
    width = emb_grads.shape[1]
    block_rows = 8
    e_width = block_rows * width
    count = touched.shape[1]
    slots = block_slot.shape[1]
    local_blocks = slot_table.shape[1]
    tokens = x.shape[1]
    din = x.shape[0]
    h_one, h_two = acc_two.shape
    out_dim = acc_three.shape[1]
    half_one, half_two = h_one // 2, h_two // 2
    fold_two = half_one // places // 8
    fold_three = half_two // places // 8

    barrier = pltpu.get_barrier_semaphore()

    def greet(device):
        pl.semaphore_signal(barrier, inc=1, device_id=device, device_id_type=MESH)

    pairs = [
        (touched_in, touched),
        (block_slot_in, block_slot),
        (emb_in, emb_grads),
        (ins[3], o_w[0]),
        (ins[4], o_w[1]),
        (ins[5], o_w[2]),
        (x_in, x),
        (cot_in, cot),
        (slot_table_in, slot_table),
        (ins[0], o_table),
        (ins[1], o_first),
        (ins[2], o_second),
    ] + list(zip(ins[6:], outs[6:]))
    loads = [pltpu.make_async_copy(a, b, load_sem.at[i]) for i, (a, b) in enumerate(pairs)]
    for d in loads[:3]:
        d.start()
    for k in range(1, shards):
        greet((g, lax.rem(s + k, shards)))
    for k in range(1, grps):
        greet((lax.rem(g + k, grps), s))
    for d in loads[3:8]:
        d.start()

    def remote(src, dst, ssem, rsem, device):
        return pltpu.make_async_remote_copy(
            src_ref=src,
            dst_ref=dst,
            send_sem=ssem,
            recv_sem=rsem,
            device_id=device,
            device_id_type=MESH,
        )

    def plane(phase, k, src, dst):
        device = (g, lax.rem(s + k, shards))
        return remote(src, dst, plane_ssem.at[phase, k], plane_rsem.at[phase, k], device)

    def along(phase, k, src, dst):
        device = (lax.rem(g + k, grps), s)
        return remote(src, dst, z_ssem.at[phase, k], z_rsem.at[phase, k], device)

    def other(phase, src, dst):
        return remote(src, dst, core_ssem.at[phase], core_rsem.at[phase], (g, s + 1 - 2 * c))

    def place(phase, k, src, dst):
        device = (g, 2 * lax.rem(p + k, places) + c)
        return remote(src, dst, plane_ssem.at[phase, k], plane_rsem.at[phase, k], device)

    sends = []

    def start(copies):
        for d in copies:
            d.start()
        sends.extend(copies)
        return copies

    def z_spread(phase, buf):
        return start([along(phase, k, buf.at[g], buf.at[g]) for k in range(1, grps)])

    def recv(copies):
        for d in copies:
            d.wait_recv()

    def total(buf, n, *at):
        out = buf[(0,) + at].astype(F32)
        for i in range(1, n):
            out += buf[(i,) + at].astype(F32)
        return out

    for d in loads[:3]:
        d.wait()
    eye = square_eye(count)
    touched_col = to_col(touched[...].astype(F32), eye)
    hot = touched_col == iota((count, slots), 1)
    slot_col = jnp.sum(jnp.where(hot, block_slot[...].astype(F32), 0.0), axis=1, keepdims=True)
    slot_row = to_row(slot_col, eye)
    owner_col = jnp.floor((slot_col + 0.5) / local_blocks)
    owner_row = jnp.floor((slot_row + 0.5) / local_blocks)
    local_row = slot_row - owner_row * local_blocks
    earlier = (owner_col == owner_row) & (iota((count, count), 0) < iota((count, count), 1))
    rank_row = jnp.sum(jnp.where(earlier, 1.0, 0.0), axis=0, keepdims=True)
    send_row = owner_row * CAP + rank_row
    picker = iota((shards * CAP, count), 0) == send_row
    pick_f32 = jnp.where(picker, 1.0, 0.0)
    pick_bf = pick_f32.astype(BF16)
    filled = jnp.sum(pick_f32, axis=1, keepdims=True)
    local_col = jnp.sum(jnp.where(picker, local_row, 0.0), axis=1, keepdims=True)
    local_col = jnp.where(filled > 0.5, local_col, -1.0)
    rows_f32[...] = emb_grads[...].astype(F32)
    for r in range(block_rows):
        part = rows_f32[pl.ds(r, count, stride=block_rows), :].astype(BF16)
        picked = mm(pick_bf, part).reshape(shards, CAP, width)
        e_send[:, :, r * width : (r + 1) * width] = picked.astype(BF16)
    lanes = jnp.broadcast_to(local_col, (shards * CAP, width)).reshape(shards, CAP, width)
    t_send[...] = lanes.astype(BF16)
    e_recv[g, s] = e_send[s]
    t_recv[s] = t_send[s]

    for d in loads[3:6]:
        d.wait()
    w1t[...] = o_w[0][...].T.astype(BF16)
    w2t[...] = o_w[1][...].T.astype(BF16)
    w2b[...] = o_w[1][...].astype(BF16)
    w3b[...] = o_w[2][...].astype(BF16)
    acc_one[...] = jnp.zeros_like(acc_one)
    acc_two[...] = jnp.zeros_like(acc_two)
    acc_three[...] = jnp.zeros_like(acc_three)

    pl.semaphore_wait(barrier, shards + grps - 2)
    t_plane = start(
        [plane(2, k, t_send.at[lax.rem(s + k, shards)], t_recv.at[s]) for k in range(1, shards)]
    )
    e_plane = start(
        [plane(3, k, e_send.at[lax.rem(s + k, shards)], e_recv.at[g, s]) for k in range(1, shards)]
    )

    for d in loads[6:8]:
        d.wait()
    for d in loads[8:]:
        d.start()

    def forward(i, carry):
        tok = pl.ds(pl.multiple_of(i * chunk, chunk), chunk)
        pre = mm(w1t[...], x[:, tok])
        logistic = 0.5 * jnp.tanh(0.5 * pre) + 0.5
        slope_buf[:, tok] = logistic
        hidden_one = (pre * logistic).astype(BF16)
        hidden_buf[:, tok] = hidden_one
        hid, slope = gate(mm(w2t[...], hidden_one))
        cc = cot[tok, :]
        acc_three[...] += mm(hid.astype(BF16), cc)
        back = (mm(w3b[...], cc, NT) * slope).astype(BF16)
        back_buf[:, tok] = back
        acc_two[...] += mm(hidden_one, back, NT)
        return carry

    back_chunk = min(1024, tokens)
    back_steps = tokens // back_chunk

    def backward(i, carry):
        tok = pl.ds(pl.multiple_of(i * back_chunk, back_chunk), back_chunk)
        logistic = slope_buf[:, tok]
        slope = logistic + hidden_buf[:, tok].astype(F32) * (1.0 - logistic)
        back = (mm(w2b[...], back_buf[:, tok]) * slope).astype(BF16)
        acc_one[0:din, :] += mm(x[:, tok], back, NT)
        return carry

    steps = tokens // chunk
    lead = min(HEAD, steps)
    lax.fori_loop(0, lead, forward, 0)
    recv(t_plane)
    group = shards * CAP
    tag_lanes = t_all.shape[2]
    tag_eye = iota((group, tag_lanes), 0) == iota((group, tag_lanes), 1)
    tag_row = to_row(t_recv[...].astype(F32).reshape(group, width)[:, 0:1], tag_eye)
    t_all[g] = jnp.broadcast_to(tag_row, t_all.shape[1:]).astype(BF16)
    t_z = z_spread(1, t_all)
    recv(e_plane)
    e_z = z_spread(2, e_recv)
    lax.fori_loop(lead, steps, forward, 0)

    base = fold_two * h_two

    def folded(part):
        two = acc_two[pl.ds(pl.multiple_of(part * half_one, half_one), half_one), :]
        three = acc_three[pl.ds(pl.multiple_of(part * half_two, half_two), half_two), :]
        two = two.reshape(places, fold_two * 8, h_two)
        three = three.reshape(places, fold_three * 8, out_dim)
        out = [(a * h_two, two[:, 8 * a : 8 * a + 8, :]) for a in range(fold_two)]
        return out + [
            (base + b * out_dim, three[:, 8 * b : 8 * b + 8, :]) for b in range(fold_three)
        ]

    for at, piece in folded(1 - c):
        p_send[:, :, at : at + piece.shape[2]] = piece.astype(BF16)
    c_p = start([other(0, p_send, p_recv)])
    late = max(0, back_steps - TAIL)
    lax.fori_loop(0, late, backward, 0)
    recv(c_p)
    for at, piece in folded(c):
        there = p_recv[:, :, at : at + piece.shape[2]].astype(F32)
        q_send[:, :, at : at + piece.shape[2]] = (piece + there).astype(BF16)

    c_r = start(
        [place(4, k, q_send.at[lax.rem(p + k, places)], r_recv.at[p]) for k in range(1, places)]
    )
    r_recv[p] = q_send[p]

    lax.fori_loop(late, back_steps, backward, 0)
    thin = acc_one.shape[0] // 2
    my_rows = pl.ds(pl.multiple_of(c * thin, thin), thin)
    its_rows = pl.ds(pl.multiple_of((1 - c) * thin, thin), thin)
    c_s = start([other(1, acc_one.at[its_rows], s_recv)])

    for d in loads[8:]:
        d.wait()
    slot_eye = square_eye(local_blocks)
    table_col = to_col(slot_table[...].astype(F32), slot_eye)
    table_hot = table_col == iota((local_blocks, 128), 1)
    row_weight = jnp.zeros((local_blocks, width), F32)
    for r in range(block_rows):
        weight = o_table[pl.ds(r, local_blocks, stride=block_rows), :]
        row_weight += weight * weight
    weight_col = jnp.sum(row_weight, axis=1, keepdims=True)
    weight_row = jnp.sum(jnp.where(table_hot, weight_col, 0.0), axis=0, keepdims=True)

    recv(c_s)
    y_plane[p] = (acc_one[my_rows, :] + s_recv[...]).astype(BF16)
    c_yp = start([place(1, k, y_plane.at[p], y_plane.at[p]) for k in range(1, places)])
    recv(c_r)
    r_line[g] = total(r_recv, places).astype(BF16)
    c_rz = z_spread(3, r_line)

    recv(c_yp)
    y_z[g] = total(y_plane, places).astype(BF16)
    c_yz = z_spread(0, y_z)

    entries = grps * group
    slots_at = iota((local_blocks, group), 0)
    recv(t_z)
    matches = []
    for q in range(grps):
        tags = t_all[q, 0:1, 0:group].astype(F32)
        matches.append(jnp.where(slots_at == tags, 1.0, 0.0))
    hits = jnp.sum(sum(matches), axis=1, keepdims=True) > 0.5
    mask = jnp.broadcast_to(jnp.where(hits, 1.0, 0.0), (local_blocks, width)) > 0.5
    match_t = jnp.concatenate(matches, axis=1).astype(BF16)
    recv(e_z)
    row_update = jnp.zeros((local_blocks, width), F32)
    for r in range(block_rows):
        at = pl.ds(r, local_blocks, stride=block_rows)
        rows = e_recv[:, :, :, r * width : (r + 1) * width].astype(F32)
        summed = mm(match_t, rows.reshape(entries, width).astype(BF16))
        first_old, second_old = o_first[at, :], o_second[at, :]
        first, second, update = adam(first_old, second_old, summed, o_table[at, :])
        update = jnp.where(mask, update, 0.0)
        o_first[at, :] = jnp.where(mask, first, first_old)
        o_second[at, :] = jnp.where(mask, second, second_old)
        table_update[at, :] = update
        row_update += update * update
    update_col = jnp.sum(row_update, axis=1, keepdims=True)
    update_row = jnp.sum(jnp.where(table_hot, update_col, 0.0), axis=0, keepdims=True)
    stats[s] = jnp.concatenate([weight_row, update_row, jnp.zeros((6, 128), F32)], axis=0)
    c_st = start([plane(0, k, stats.at[s], stats.at[s]) for k in range(1, shards)])

    recv(c_rz)
    a_all[c, p] = total(r_line, grps).astype(BF16)
    c_ap = start([place(5, k, a_all.at[c, p], a_all.at[c, p]) for k in range(1, places)])
    recv(c_yz)
    y_all[c] = total(y_z, grps)
    c_y = start([other(2, y_all.at[c], y_all.at[c])])
    weight_sq = [jnp.sum(w[...] * w[...], keepdims=True) for w in o_w]

    recv(c_ap)
    c_a = start([other(3, a_all.at[c], a_all.at[c])])

    def dense_step(j, rows, grad, keep):
        first, second, update = adam(o_m[j][rows, :], o_v[j][rows, :], grad, o_w[j][rows, :])
        o_m[j][rows, :] = first
        o_v[j][rows, :] = second
        if keep is not None:
            keep[rows, :] = update
        return update, jnp.sum(update * update, axis=0, keepdims=True)

    def half_step(part):
        two = [
            a_all[part, :, :, a * h_two : (a + 1) * h_two].astype(F32) for a in range(fold_two)
        ]
        three = [
            a_all[part, :, :, base + b * out_dim : base + (b + 1) * out_dim].astype(F32)
            for b in range(fold_three)
        ]
        two = jnp.concatenate(two, axis=1).reshape(half_one, h_two)
        three = jnp.concatenate(three, axis=1).reshape(half_two, out_dim)
        rows_two = pl.ds(pl.multiple_of(part * half_one, half_one), half_one)
        rows_three = pl.ds(pl.multiple_of(part * half_two, half_two), half_two)
        return (
            dense_step(1, rows_two, two, update_two)[1],
            dense_step(2, rows_three, three, update_three)[1],
        )

    def trust(j, update_sq):
        return (
            learn_rate
            * jnp.sqrt(weight_sq[j])
            / (jnp.sqrt(jnp.sum(update_sq, keepdims=True)) + ratio_eps)
        )

    here = half_step(c)
    recv(c_y)
    grad = y_all[...].reshape(2 * thin, h_one)[0:din, :]
    update, update_sq = dense_step(0, slice(None), grad, None)
    o_w[0][...] = o_w[0][...] - trust(0, update_sq) * update

    recv(c_st)
    tot = total(stats, shards)
    ratio = jnp.sqrt(tot[0:1]) / (jnp.sqrt(tot[1:2]) + ratio_eps)
    ratio_col = jnp.sum(jnp.where(table_hot, ratio, 0.0), axis=1, keepdims=True)
    rate = jnp.broadcast_to(learn_rate * ratio_col, (local_blocks, width))
    for r in range(block_rows):
        at = pl.ds(r, local_blocks, stride=block_rows)
        o_table[at, :] = o_table[at, :] - rate * table_update[at, :]

    recv(c_a)
    there = half_step(1 - c)
    o_w[1][...] = o_w[1][...] - trust(1, here[0] + there[0]) * update_two[...]
    o_w[2][...] = o_w[2][...] - trust(2, here[1] + there[1]) * update_three[...]

    for d in sends:
        d.wait_send()


def store_kernel(*refs):
    srcs, outs, sem = refs[:12], refs[12:24], refs[24]
    stores = [pltpu.make_async_copy(a, b, sem.at[i]) for i, (a, b) in enumerate(zip(srcs, outs))]
    for d in stores:
        d.start()
    for d in stores:
        d.wait()


def body(
    table, table_first, table_second, slot_table, touched, emb_grads, block_slot,
    dense_x, dense_cot, *dense,
):
    shards = lax.axis_size("shard")
    grps = lax.axis_size("grp")
    blocks, block_rows, width = table.shape
    count = touched.shape[1]
    din, tokens = dense_x.shape
    h_one, h_two = dense[1].shape
    out_dim = dense[2].shape[1]
    chunk = min(1024, tokens)
    din_pad = -(-din // 16) * 16
    flat = (blocks * block_rows, width)
    e_width = block_rows * width
    places = shards // 2
    fold = (h_one // (16 * places)) * h_two + (h_two // (16 * places)) * out_dim
    hbm = pl.BlockSpec(memory_space=pltpu.HBM)
    vmem = pl.BlockSpec(memory_space=pltpu.VMEM)
    sds = jax.ShapeDtypeStruct
    state = tuple(a.reshape(flat) for a in (table, table_first, table_second)) + dense
    shapes = tuple(sds(a.shape, F32) for a in state)
    held = pl.pallas_call(
        functools.partial(exchange_kernel, grps, shards, chunk),
        out_shape=tuple(pltpu.VMEM(a.shape, F32) for a in state),
        in_specs=[hbm] * 18,
        out_specs=(vmem,) * 12,
        scratch_shapes=[
            pltpu.VMEM((1, count), jnp.int32),
            pltpu.VMEM((1, block_slot.shape[0]), jnp.int32),
            pltpu.VMEM((1, blocks), jnp.int32),
            pltpu.VMEM((count * block_rows, width), BF16),
            pltpu.VMEM(dense_x.shape, BF16),
            pltpu.VMEM(dense_cot.shape, BF16),
            pltpu.VMEM((h_one, din), BF16),
            pltpu.VMEM((h_two, h_one), BF16),
            pltpu.VMEM((h_one, h_two), BF16),
            pltpu.VMEM((h_two, out_dim), BF16),
            pltpu.VMEM((h_one, tokens), F32),
            pltpu.VMEM((h_one, tokens), BF16),
            pltpu.VMEM((h_two, tokens), BF16),
            pltpu.VMEM((din_pad, h_one), F32),
            pltpu.VMEM((h_one, h_two), F32),
            pltpu.VMEM((h_two, out_dim), F32),
            pltpu.VMEM((count * block_rows, width), F32),
            pltpu.VMEM(flat, F32),
            pltpu.VMEM((h_one, h_two), F32),
            pltpu.VMEM((h_two, out_dim), F32),
            pltpu.VMEM((shards, CAP, e_width), BF16),
            pltpu.VMEM((grps, shards, CAP, e_width), BF16),
            pltpu.VMEM((shards, CAP, width), BF16),
            pltpu.VMEM((shards, CAP, width), BF16),
            pltpu.VMEM((grps, 16, max(128, shards * CAP)), BF16),
            pltpu.VMEM((places, 8, fold), BF16),
            pltpu.VMEM((places, 8, fold), BF16),
            pltpu.VMEM((places, 8, fold), BF16),
            pltpu.VMEM((places, 8, fold), BF16),
            pltpu.VMEM((grps, 8, fold), BF16),
            pltpu.VMEM((2, places, 8, fold), BF16),
            pltpu.VMEM((din_pad // 2, h_one), F32),
            pltpu.VMEM((places, din_pad // 2, h_one), BF16),
            pltpu.VMEM((grps, din_pad // 2, h_one), BF16),
            pltpu.VMEM((2, din_pad // 2, h_one), F32),
            pltpu.VMEM((shards, 8, 128), F32),
            pltpu.SemaphoreType.DMA((6, shards)),
            pltpu.SemaphoreType.DMA((6, shards)),
            pltpu.SemaphoreType.DMA((4, grps)),
            pltpu.SemaphoreType.DMA((4, grps)),
            pltpu.SemaphoreType.DMA((4,)),
            pltpu.SemaphoreType.DMA((4,)),
            pltpu.SemaphoreType.DMA((18,)),
        ],
        compiler_params=pltpu.CompilerParams(
            collective_id=0, has_side_effects=True, vmem_limit_bytes=44 << 20
        ),
        name="tower_exchange",
    )(
        *(
            pltpu.with_memory_space_constraint(a, pltpu.HBM)
            for a in (
                touched,
                block_slot.reshape(1, -1),
                slot_table.reshape(1, -1),
                emb_grads.reshape(count * block_rows, width),
                dense_x,
                dense_cot,
            )
            + state
        )
    )
    outs = pl.pallas_call(
        store_kernel,
        out_shape=shapes,
        in_specs=[vmem] * 12,
        out_specs=(pl.BlockSpec(memory_space=pl.ANY),) * 12,
        scratch_shapes=[pltpu.SemaphoreType.DMA((12,))],
        compiler_params=pltpu.CompilerParams(vmem_limit_bytes=12 << 20),
        name="store",
    )(*held)
    return tuple(o.reshape(table.shape) for o in outs[:3]) + tuple(outs[3:])


def solution(mesh):
    dense = (P(),) * 9
    rows = P("shard", None, None)
    return jax.shard_map(
        body,
        mesh=mesh,
        in_specs=(
            rows,
            rows,
            rows,
            P("shard"),
            P("grp", "shard"),
            P("grp", "shard", None, None),
            P(),
            P(None, ("grp", "shard")),
            P(("grp", "shard"), None),
        )
        + dense,
        out_specs=(rows,) * 3 + dense,
        check_vma=False,
    )
```

```python
import functools
import jax
import jax.numpy as jnp
from jax import lax
from jax.experimental import pallas as pl
from jax.experimental.pallas import tpu as pltpu
from jax.sharding import PartitionSpec as P

TABLES = 26
CAP = 8
TAIL = 3

beta_one = 0.9
beta_two = 0.999
corr_first = 1.0 - 0.9**10
corr_second = 1.0 - 0.999**10
adam_eps = 1e-06
decay_rate = 0.01
learn_rate = 0.1
ratio_eps = 1e-06

MESH = pl.DeviceIdType.MESH
F32 = jnp.float32
BF16 = jnp.bfloat16
NN = (((1,), (0,)), ((), ()))
NT = (((1,), (1,)), ((), ()))
TN = (((0,), (0,)), ((), ()))


def mm(a, b, dims=NN):
    return lax.dot_general(a, b, dims, preferred_element_type=F32)


def iota(shape, axis):
    return lax.broadcasted_iota(jnp.int32, shape, axis).astype(F32)


def to_col(row, eye):
    return jnp.sum(jnp.where(eye, row, 0.0), axis=1, keepdims=True)


def to_row(col, eye):
    return jnp.sum(jnp.where(eye, col, 0.0), axis=0, keepdims=True)


def square_eye(count):
    return iota((count, count), 0) == iota((count, count), 1)


def gate(pre):
    logistic = 0.5 * jnp.tanh(0.5 * pre) + 0.5
    hidden = pre * logistic
    return hidden, logistic + hidden * (1.0 - logistic)


def adam(first_in, second_in, gradient, weight):
    first_out = beta_one * first_in + (1.0 - beta_one) * gradient
    second_out = beta_two * second_in + (1.0 - beta_two) * gradient * gradient
    update = (
        first_out / corr_first / (jnp.sqrt(second_out / corr_second) + adam_eps)
        + decay_rate * weight
    )
    return first_out, second_out, update


def exchange_kernel(
    grps,
    shards,
    chunk,
    touched_in,
    block_slot_in,
    slot_table_in,
    emb_in,
    x_in,
    cot_in,
    *refs,
):
    ins, refs = refs[:12], refs[12:]
    outs, refs = refs[:12], refs[12:]
    o_table, o_first, o_second = outs[:3]
    o_w, o_m, o_v = outs[3:6], outs[6:9], outs[9:12]
    (
        touched,
        block_slot,
        slot_table,
        emb_grads,
        x,
        cot,
        w1t,
        w2t,
        w2b,
        w3b,
        slope_buf,
        hidden_buf,
        back_buf,
        acc_one,
        acc_two,
        acc_three,
        rows_f32,
        raw_all,
        raw_f32,
        touched_all,
        table_update,
        update_two,
        update_three,
        e_send,
        e_recv,
        t_send,
        t_recv,
        f_send,
        f_recv,
        u_send,
        u_recv,
        p_send,
        p_recv,
        q_send,
        r_recv,
        r_plane,
        a_all,
        s_recv,
        y_plane,
        y_z,
        y_all,
        stats,
        plane_ssem,
        plane_rsem,
        z_ssem,
        z_rsem,
        core_ssem,
        core_rsem,
        load_sem,
    ) = refs
    g = lax.axis_index("grp")
    s = lax.axis_index("shard")
    c = lax.rem(s, 2)
    p = s // 2
    places = shards // 2
    width = emb_grads.shape[1]
    block_rows = 8
    e_width = block_rows * width
    count = touched.shape[1]
    slots = block_slot.shape[1]
    local_blocks = slot_table.shape[1]
    tokens = x.shape[1]
    din = x.shape[0]
    h_one, h_two = acc_two.shape
    out_dim = acc_three.shape[1]
    half_one, half_two = h_one // 2, h_two // 2
    fold_two = half_one // grps // 8
    fold_three = half_two // grps // 8

    barrier = pltpu.get_barrier_semaphore()

    def greet(device):
        pl.semaphore_signal(barrier, inc=1, device_id=device, device_id_type=MESH)

    pairs = [
        (touched_in, touched),
        (block_slot_in, block_slot),
        (emb_in, emb_grads),
        (ins[3], o_w[0]),
        (ins[4], o_w[1]),
        (ins[5], o_w[2]),
        (x_in, x),
        (cot_in, cot),
        (slot_table_in, slot_table),
        (ins[0], o_table),
        (ins[1], o_first),
        (ins[2], o_second),
    ] + list(zip(ins[6:], outs[6:]))
    loads = [pltpu.make_async_copy(a, b, load_sem.at[i]) for i, (a, b) in enumerate(pairs)]
    for d in loads[:3]:
        d.start()
    for k in range(1, shards):
        greet((g, lax.rem(s + k, shards)))
    for k in range(1, grps):
        greet((lax.rem(g + k, grps), s))
    for d in loads[3:8]:
        d.start()

    def remote(src, dst, ssem, rsem, device):
        return pltpu.make_async_remote_copy(
            src_ref=src,
            dst_ref=dst,
            send_sem=ssem,
            recv_sem=rsem,
            device_id=device,
            device_id_type=MESH,
        )

    def plane(phase, k, src, dst):
        device = (g, lax.rem(s + k, shards))
        return remote(src, dst, plane_ssem.at[phase, k], plane_rsem.at[phase, k], device)

    def along(phase, k, src, dst):
        device = (lax.rem(g + k, grps), s)
        return remote(src, dst, z_ssem.at[phase, k], z_rsem.at[phase, k], device)

    def other(phase, src, dst):
        return remote(src, dst, core_ssem.at[phase], core_rsem.at[phase], (g, s + 1 - 2 * c))

    def place(phase, k, src, dst):
        device = (g, 2 * lax.rem(p + k, places) + c)
        return remote(src, dst, plane_ssem.at[phase, k], plane_rsem.at[phase, k], device)

    sends = []

    def start(copies):
        for d in copies:
            d.start()
        sends.extend(copies)
        return copies

    def z_spread(phase, buf):
        return start([along(phase, k, buf.at[g], buf.at[g]) for k in range(1, grps)])

    def recv(copies):
        for d in copies:
            d.wait_recv()

    def total(buf, n, *at):
        out = buf[(0,) + at].astype(F32)
        for i in range(1, n):
            out += buf[(i,) + at].astype(F32)
        return out

    for d in loads[:3]:
        d.wait()
    eye = square_eye(count)

    def route(touched_col, rows_ref, out, tag_out):
        n = touched_col.shape[0]
        cap = n // count * CAP
        hot = touched_col == iota((n, slots), 1)
        slot_col = jnp.sum(jnp.where(hot, block_slot[...].astype(F32), 0.0), axis=1, keepdims=True)
        slot_row = to_row(slot_col, square_eye(n))
        owner_col = jnp.floor((slot_col + 0.5) / local_blocks)
        owner_row = jnp.floor((slot_row + 0.5) / local_blocks)
        local_row = slot_row - owner_row * local_blocks
        at_col, at_row = iota((n, n), 0), iota((n, n), 1)
        line_col = jnp.floor((at_col + 0.5) / count)
        line_row = jnp.floor((at_row + 0.5) / count)
        earlier = (owner_col == owner_row) & (line_col == line_row) & (at_col < at_row)
        rank_row = jnp.sum(jnp.where(earlier, 1.0, 0.0), axis=0, keepdims=True)
        send_row = owner_row * cap + line_row[0:1, :] * CAP + rank_row
        picker = iota((shards * cap, n), 0) == send_row
        pick_f32 = jnp.where(picker, 1.0, 0.0)
        pick_bf = pick_f32.astype(BF16)
        filled = jnp.sum(pick_f32, axis=1, keepdims=True)
        local_col = jnp.sum(jnp.where(picker, local_row, 0.0), axis=1, keepdims=True)
        local_col = jnp.where(filled > 0.5, local_col, -1.0)
        for r in range(block_rows):
            part = rows_ref[pl.ds(r, n, stride=block_rows), :].astype(BF16)
            picked = mm(pick_bf, part).reshape(shards, cap, width)
            out[:, :, r * width : (r + 1) * width] = picked.astype(BF16)
        lanes = jnp.broadcast_to(local_col, (shards * cap, local_blocks))
        tag_out[...] = lanes.reshape(shards, cap, local_blocks).astype(BF16)

    def deliver(phase, send, land):
        land[s] = send[s]
        return start(
            [plane(phase, k, send.at[lax.rem(s + k, shards)], land.at[s]) for k in range(1, shards)]
        )

    rows_f32[...] = emb_grads[...].astype(F32)
    route(to_col(touched[...].astype(F32), eye), rows_f32, e_send, t_send)

    pl.semaphore_wait(barrier, shards + grps - 2)
    raw = start([along(2, k, emb_grads, raw_all.at[g]) for k in range(1, grps)])
    raw += start([along(1, k, touched, touched_all.at[g]) for k in range(1, grps)])
    near = deliver(3, e_send, e_recv) + deliver(2, t_send, t_recv)

    for d in loads[3:6]:
        d.wait()
    w1t[...] = o_w[0][...].T.astype(BF16)
    w2t[...] = o_w[1][...].T.astype(BF16)
    w2b[...] = o_w[1][...].astype(BF16)
    w3b[...] = o_w[2][...].astype(BF16)
    acc_one[...] = jnp.zeros_like(acc_one)
    acc_two[...] = jnp.zeros_like(acc_two)
    acc_three[...] = jnp.zeros_like(acc_three)

    for d in loads[6:8]:
        d.wait()
    for d in loads[8:]:
        d.start()

    def forward(i, carry):
        tok = pl.ds(pl.multiple_of(i * chunk, chunk), chunk)
        pre = mm(w1t[...], x[:, tok])
        logistic = 0.5 * jnp.tanh(0.5 * pre) + 0.5
        slope_buf[:, tok] = logistic
        hidden_one = (pre * logistic).astype(BF16)
        hidden_buf[:, tok] = hidden_one
        hid, slope = gate(mm(w2t[...], hidden_one))
        cc = cot[tok, :]
        acc_three[...] += mm(hid.astype(BF16), cc)
        back = (mm(w3b[...], cc, NT) * slope).astype(BF16)
        back_buf[:, tok] = back
        acc_two[...] += mm(hidden_one, back, NT)
        return carry

    back_chunk = min(1024, tokens)
    back_steps = tokens // back_chunk

    def backward(i, carry):
        tok = pl.ds(pl.multiple_of(i * back_chunk, back_chunk), back_chunk)
        logistic = slope_buf[:, tok]
        slope = logistic + hidden_buf[:, tok].astype(F32) * (1.0 - logistic)
        back = (mm(w2b[...], back_buf[:, tok]) * slope).astype(BF16)
        acc_one[0:din, :] += mm(x[:, tok], back, NT)
        return carry

    steps = tokens // chunk
    lax.fori_loop(0, steps, forward, 0)

    base = fold_two * h_two

    def folded(part):
        two = acc_two[pl.ds(pl.multiple_of(part * half_one, half_one), half_one), :]
        three = acc_three[pl.ds(pl.multiple_of(part * half_two, half_two), half_two), :]
        two = two.reshape(grps, fold_two * 8, h_two)
        three = three.reshape(grps, fold_three * 8, out_dim)
        out = [(a * h_two, two[:, 8 * a : 8 * a + 8, :]) for a in range(fold_two)]
        return out + [
            (base + b * out_dim, three[:, 8 * b : 8 * b + 8, :]) for b in range(fold_three)
        ]

    for at, piece in folded(1 - c):
        p_send[:, :, at : at + piece.shape[2]] = piece.astype(BF16)
    c_p = start([other(0, p_send, p_recv)])
    recv(raw)
    cols = []
    for k in range(1, grps):
        q = lax.rem(g + k, grps)
        raw_f32[pl.ds((k - 1) * count * block_rows, count * block_rows), :] = raw_all[q].astype(F32)
        cols.append(to_col(touched_all[q].astype(F32), eye))
    route(jnp.concatenate(cols, axis=0), raw_f32, f_send, u_send)
    far = deliver(6, f_send, f_recv) + deliver(7, u_send, u_recv)
    late = max(0, back_steps - TAIL)
    lax.fori_loop(0, late, backward, 0)
    recv(c_p)
    for at, piece in folded(c):
        there = p_recv[:, :, at : at + piece.shape[2]].astype(F32)
        q_send[:, :, at : at + piece.shape[2]] = (piece + there).astype(BF16)

    c_r = start(
        [along(3, k, q_send.at[lax.rem(g + k, grps)], r_recv.at[g]) for k in range(1, grps)]
    )
    r_recv[g] = q_send[g]

    lax.fori_loop(late, back_steps, backward, 0)
    thin = acc_one.shape[0] // 2
    my_rows = pl.ds(pl.multiple_of(c * thin, thin), thin)
    its_rows = pl.ds(pl.multiple_of((1 - c) * thin, thin), thin)
    c_s = start([other(1, acc_one.at[its_rows], s_recv)])

    for d in loads[8:]:
        d.wait()
    slot_eye = square_eye(local_blocks)
    table_col = to_col(slot_table[...].astype(F32), slot_eye)
    table_hot = table_col == iota((local_blocks, 128), 1)
    row_weight = jnp.zeros((local_blocks, width), F32)
    for r in range(block_rows):
        weight = o_table[pl.ds(r, local_blocks, stride=block_rows), :]
        row_weight += weight * weight
    weight_col = jnp.sum(row_weight, axis=1, keepdims=True)
    weight_row = jnp.sum(jnp.where(table_hot, weight_col, 0.0), axis=0, keepdims=True)

    recv(c_s)
    y_plane[p] = (acc_one[my_rows, :] + s_recv[...]).astype(BF16)
    c_yp = start([place(1, k, y_plane.at[p], y_plane.at[p]) for k in range(1, places)])
    recv(c_r)
    r_plane[p] = total(r_recv, grps).astype(BF16)
    c_rp = start([place(4, k, r_plane.at[p], r_plane.at[p]) for k in range(1, places)])

    recv(c_yp)
    y_z[g] = total(y_plane, places).astype(BF16)
    c_yz = z_spread(0, y_z)

    recv(near)
    recv(far)
    tags = jnp.concatenate(
        [
            t_recv[...].astype(F32).reshape(shards * CAP, local_blocks),
            u_recv[...].astype(F32).reshape(shards * (grps - 1) * CAP, local_blocks),
        ],
        axis=0,
    )
    match_f32 = jnp.where(tags == iota(tags.shape, 1), 1.0, 0.0)
    match_t = match_f32.T.astype(BF16)
    hits = to_col(jnp.sum(match_f32, axis=0, keepdims=True), slot_eye) > 0.5
    mask = jnp.broadcast_to(jnp.where(hits, 1.0, 0.0), (local_blocks, width)) > 0.5
    row_update = jnp.zeros((local_blocks, width), F32)
    for r in range(block_rows):
        at = pl.ds(r, local_blocks, stride=block_rows)
        lanes = slice(r * width, (r + 1) * width)
        rows_near = e_recv[:, :, lanes].astype(F32).reshape(shards * CAP, width)
        rows_far = f_recv[:, :, lanes].astype(F32).reshape(shards * (grps - 1) * CAP, width)
        summed = mm(match_t, jnp.concatenate([rows_near, rows_far], axis=0).astype(BF16))
        first_old, second_old = o_first[at, :], o_second[at, :]
        first, second, update = adam(first_old, second_old, summed, o_table[at, :])
        update = jnp.where(mask, update, 0.0)
        o_first[at, :] = jnp.where(mask, first, first_old)
        o_second[at, :] = jnp.where(mask, second, second_old)
        table_update[at, :] = update
        row_update += update * update
    update_col = jnp.sum(row_update, axis=1, keepdims=True)
    update_row = jnp.sum(jnp.where(table_hot, update_col, 0.0), axis=0, keepdims=True)
    stats[s] = jnp.concatenate([weight_row, update_row, jnp.zeros((6, 128), F32)], axis=0)
    c_st = start([plane(0, k, stats.at[s], stats.at[s]) for k in range(1, shards)])

    recv(c_rp)
    a_all[c, g] = total(r_plane, places).astype(BF16)
    c_ap = start([along(4, k, a_all.at[c, g], a_all.at[c, g]) for k in range(1, grps)])
    recv(c_yz)
    y_all[c] = total(y_z, grps)
    c_y = start([other(2, y_all.at[c], y_all.at[c])])
    weight_sq = [jnp.sum(w[...] * w[...], keepdims=True) for w in o_w]

    recv(c_ap)
    c_a = start([other(3, a_all.at[c], a_all.at[c])])

    def dense_step(j, rows, grad, keep):
        first, second, update = adam(o_m[j][rows, :], o_v[j][rows, :], grad, o_w[j][rows, :])
        o_m[j][rows, :] = first
        o_v[j][rows, :] = second
        if keep is not None:
            keep[rows, :] = update
        return update, jnp.sum(update * update, axis=0, keepdims=True)

    def half_step(part):
        two = [
            a_all[part, :, :, a * h_two : (a + 1) * h_two].astype(F32) for a in range(fold_two)
        ]
        three = [
            a_all[part, :, :, base + b * out_dim : base + (b + 1) * out_dim].astype(F32)
            for b in range(fold_three)
        ]
        two = jnp.concatenate(two, axis=1).reshape(half_one, h_two)
        three = jnp.concatenate(three, axis=1).reshape(half_two, out_dim)
        rows_two = pl.ds(pl.multiple_of(part * half_one, half_one), half_one)
        rows_three = pl.ds(pl.multiple_of(part * half_two, half_two), half_two)
        return (
            dense_step(1, rows_two, two, update_two)[1],
            dense_step(2, rows_three, three, update_three)[1],
        )

    def trust(j, update_sq):
        return (
            learn_rate
            * jnp.sqrt(weight_sq[j])
            / (jnp.sqrt(jnp.sum(update_sq, keepdims=True)) + ratio_eps)
        )

    here = half_step(c)
    recv(c_y)
    grad = y_all[...].reshape(2 * thin, h_one)[0:din, :]
    update, update_sq = dense_step(0, slice(None), grad, None)
    o_w[0][...] = o_w[0][...] - trust(0, update_sq) * update

    recv(c_st)
    tot = total(stats, shards)
    ratio = jnp.sqrt(tot[0:1]) / (jnp.sqrt(tot[1:2]) + ratio_eps)
    ratio_col = jnp.sum(jnp.where(table_hot, ratio, 0.0), axis=1, keepdims=True)
    rate = jnp.broadcast_to(learn_rate * ratio_col, (local_blocks, width))
    for r in range(block_rows):
        at = pl.ds(r, local_blocks, stride=block_rows)
        o_table[at, :] = o_table[at, :] - rate * table_update[at, :]

    recv(c_a)
    there = half_step(1 - c)
    o_w[1][...] = o_w[1][...] - trust(1, here[0] + there[0]) * update_two[...]
    o_w[2][...] = o_w[2][...] - trust(2, here[1] + there[1]) * update_three[...]

    for d in sends:
        d.wait_send()


def store_kernel(*refs):
    srcs, outs, sem = refs[:12], refs[12:24], refs[24]
    stores = [pltpu.make_async_copy(a, b, sem.at[i]) for i, (a, b) in enumerate(zip(srcs, outs))]
    for d in stores:
        d.start()
    for d in stores:
        d.wait()


def body(
    table, table_first, table_second, slot_table, touched, emb_grads, block_slot,
    dense_x, dense_cot, *dense,
):
    shards = lax.axis_size("shard")
    grps = lax.axis_size("grp")
    blocks, block_rows, width = table.shape
    count = touched.shape[1]
    din, tokens = dense_x.shape
    h_one, h_two = dense[1].shape
    out_dim = dense[2].shape[1]
    chunk = min(1024, tokens)
    din_pad = -(-din // 16) * 16
    flat = (blocks * block_rows, width)
    e_width = block_rows * width
    places = shards // 2
    fold = (h_one // (16 * grps)) * h_two + (h_two // (16 * grps)) * out_dim
    hbm = pl.BlockSpec(memory_space=pltpu.HBM)
    vmem = pl.BlockSpec(memory_space=pltpu.VMEM)
    sds = jax.ShapeDtypeStruct
    state = tuple(a.reshape(flat) for a in (table, table_first, table_second)) + dense
    shapes = tuple(sds(a.shape, F32) for a in state)
    held = pl.pallas_call(
        functools.partial(exchange_kernel, grps, shards, chunk),
        out_shape=tuple(pltpu.VMEM(a.shape, F32) for a in state),
        in_specs=[hbm] * 18,
        out_specs=(vmem,) * 12,
        scratch_shapes=[
            pltpu.VMEM((1, count), jnp.int32),
            pltpu.VMEM((1, block_slot.shape[0]), jnp.int32),
            pltpu.VMEM((1, blocks), jnp.int32),
            pltpu.VMEM((count * block_rows, width), BF16),
            pltpu.VMEM(dense_x.shape, BF16),
            pltpu.VMEM(dense_cot.shape, BF16),
            pltpu.VMEM((h_one, din), BF16),
            pltpu.VMEM((h_two, h_one), BF16),
            pltpu.VMEM((h_one, h_two), BF16),
            pltpu.VMEM((h_two, out_dim), BF16),
            pltpu.VMEM((h_one, tokens), F32),
            pltpu.VMEM((h_one, tokens), BF16),
            pltpu.VMEM((h_two, tokens), BF16),
            pltpu.VMEM((din_pad, h_one), F32),
            pltpu.VMEM((h_one, h_two), F32),
            pltpu.VMEM((h_two, out_dim), F32),
            pltpu.VMEM((count * block_rows, width), F32),
            pltpu.VMEM((grps, count * block_rows, width), BF16),
            pltpu.VMEM(((grps - 1) * count * block_rows, width), F32),
            pltpu.VMEM((grps, 1, count), jnp.int32),
            pltpu.VMEM(flat, F32),
            pltpu.VMEM((h_one, h_two), F32),
            pltpu.VMEM((h_two, out_dim), F32),
            pltpu.VMEM((shards, CAP, e_width), BF16),
            pltpu.VMEM((shards, CAP, e_width), BF16),
            pltpu.VMEM((shards, CAP, blocks), BF16),
            pltpu.VMEM((shards, CAP, blocks), BF16),
            pltpu.VMEM((shards, (grps - 1) * CAP, e_width), BF16),
            pltpu.VMEM((shards, (grps - 1) * CAP, e_width), BF16),
            pltpu.VMEM((shards, (grps - 1) * CAP, blocks), BF16),
            pltpu.VMEM((shards, (grps - 1) * CAP, blocks), BF16),
            pltpu.VMEM((grps, 8, fold), BF16),
            pltpu.VMEM((grps, 8, fold), BF16),
            pltpu.VMEM((grps, 8, fold), BF16),
            pltpu.VMEM((grps, 8, fold), BF16),
            pltpu.VMEM((places, 8, fold), BF16),
            pltpu.VMEM((2, grps, 8, fold), BF16),
            pltpu.VMEM((din_pad // 2, h_one), F32),
            pltpu.VMEM((places, din_pad // 2, h_one), BF16),
            pltpu.VMEM((grps, din_pad // 2, h_one), BF16),
            pltpu.VMEM((2, din_pad // 2, h_one), F32),
            pltpu.VMEM((shards, 8, 128), F32),
            pltpu.SemaphoreType.DMA((8, shards)),
            pltpu.SemaphoreType.DMA((8, shards)),
            pltpu.SemaphoreType.DMA((5, grps)),
            pltpu.SemaphoreType.DMA((5, grps)),
            pltpu.SemaphoreType.DMA((4,)),
            pltpu.SemaphoreType.DMA((4,)),
            pltpu.SemaphoreType.DMA((18,)),
        ],
        compiler_params=pltpu.CompilerParams(
            collective_id=0, has_side_effects=True, vmem_limit_bytes=44 << 20
        ),
        name="tower_exchange",
    )(
        *(
            pltpu.with_memory_space_constraint(a, pltpu.HBM)
            for a in (
                touched,
                block_slot.reshape(1, -1),
                slot_table.reshape(1, -1),
                emb_grads.reshape(count * block_rows, width),
                dense_x,
                dense_cot,
            )
            + state
        )
    )
    outs = pl.pallas_call(
        store_kernel,
        out_shape=shapes,
        in_specs=[vmem] * 12,
        out_specs=(pl.BlockSpec(memory_space=pl.ANY),) * 12,
        scratch_shapes=[pltpu.SemaphoreType.DMA((12,))],
        compiler_params=pltpu.CompilerParams(vmem_limit_bytes=12 << 20),
        name="store",
    )(*held)
    return tuple(o.reshape(table.shape) for o in outs[:3]) + tuple(outs[3:])


def solution(mesh):
    dense = (P(),) * 9
    rows = P("shard", None, None)
    return jax.shard_map(
        body,
        mesh=mesh,
        in_specs=(
            rows,
            rows,
            rows,
            P("shard"),
            P("grp", "shard"),
            P("grp", "shard", None, None),
            P(),
            P(None, ("grp", "shard")),
            P(("grp", "shard"), None),
        )
        + dense,
        out_specs=(rows,) * 3 + dense,
        check_vma=False,
    )
```

```python
import functools
import jax
import jax.numpy as jnp
from jax import lax
from jax.experimental import pallas as pl
from jax.experimental.pallas import tpu as pltpu
from jax.sharding import PartitionSpec as P

TABLES = 26
CAP = 8
TAIL = 3

beta_one = 0.9
beta_two = 0.999
corr_first = 1.0 - 0.9**10
corr_second = 1.0 - 0.999**10
adam_eps = 1e-06
decay_rate = 0.01
learn_rate = 0.1
ratio_eps = 1e-06

MESH = pl.DeviceIdType.MESH
F32 = jnp.float32
BF16 = jnp.bfloat16
NN = (((1,), (0,)), ((), ()))
NT = (((1,), (1,)), ((), ()))
TN = (((0,), (0,)), ((), ()))


def mm(a, b, dims=NN):
    return lax.dot_general(a, b, dims, preferred_element_type=F32)


def iota(shape, axis):
    return lax.broadcasted_iota(jnp.int32, shape, axis).astype(F32)


def to_col(row, eye):
    return jnp.sum(jnp.where(eye, row, 0.0), axis=1, keepdims=True)


def to_row(col, eye):
    return jnp.sum(jnp.where(eye, col, 0.0), axis=0, keepdims=True)


def square_eye(count):
    return iota((count, count), 0) == iota((count, count), 1)


def gate(pre):
    logistic = 0.5 * jnp.tanh(0.5 * pre) + 0.5
    hidden = pre * logistic
    return hidden, logistic + hidden * (1.0 - logistic)


def adam(first_in, second_in, gradient, weight):
    first_out = beta_one * first_in + (1.0 - beta_one) * gradient
    second_out = beta_two * second_in + (1.0 - beta_two) * gradient * gradient
    update = (
        first_out / corr_first / (jnp.sqrt(second_out / corr_second) + adam_eps)
        + decay_rate * weight
    )
    return first_out, second_out, update


def exchange_kernel(
    grps,
    shards,
    chunk,
    touched_in,
    block_slot_in,
    slot_table_in,
    emb_in,
    x_in,
    cot_in,
    *refs,
):
    ins, refs = refs[:12], refs[12:]
    outs, refs = refs[:12], refs[12:]
    o_table, o_first, o_second = outs[:3]
    o_w, o_m, o_v = outs[3:6], outs[6:9], outs[9:12]
    (
        touched,
        block_slot,
        slot_table,
        emb_grads,
        x,
        cot,
        w1t,
        w2t,
        w2b,
        w3b,
        slope_buf,
        hidden_buf,
        back_buf,
        acc_one,
        acc_two,
        acc_three,
        rows_f32,
        raw_all,
        raw_f32,
        touched_all,
        table_update,
        update_two,
        update_three,
        e_send,
        e_recv,
        t_send,
        t_recv,
        f_send,
        f_recv,
        u_send,
        u_recv,
        p_send,
        p_recv,
        q_send,
        r_recv,
        r_plane,
        a_all,
        s_recv,
        y_plane,
        y_z,
        y_all,
        stats,
        plane_ssem,
        plane_rsem,
        z_ssem,
        z_rsem,
        core_ssem,
        core_rsem,
        load_sem,
    ) = refs
    g = lax.axis_index("grp")
    s = lax.axis_index("shard")
    c = lax.rem(s, 2)
    p = s // 2
    places = shards // 2
    width = emb_grads.shape[1]
    block_rows = 8
    e_width = block_rows * width
    count = touched.shape[1]
    slots = block_slot.shape[1]
    local_blocks = slot_table.shape[1]
    tokens = x.shape[1]
    din = x.shape[0]
    h_one, h_two = acc_two.shape
    out_dim = acc_three.shape[1]
    half_one, half_two = h_one // 2, h_two // 2
    fold_two = half_one // grps // 8
    fold_three = half_two // grps // 8

    barrier = pltpu.get_barrier_semaphore()

    def greet(device):
        pl.semaphore_signal(barrier, inc=1, device_id=device, device_id_type=MESH)

    pairs = [
        (touched_in, touched),
        (block_slot_in, block_slot),
        (emb_in, emb_grads),
        (ins[3], o_w[0]),
        (ins[4], o_w[1]),
        (ins[5], o_w[2]),
        (x_in, x),
        (cot_in, cot),
        (slot_table_in, slot_table),
        (ins[0], o_table),
        (ins[1], o_first),
        (ins[2], o_second),
    ] + list(zip(ins[6:], outs[6:]))
    loads = [pltpu.make_async_copy(a, b, load_sem.at[i]) for i, (a, b) in enumerate(pairs)]
    for d in loads[:3]:
        d.start()
    for k in range(1, shards):
        greet((g, lax.rem(s + k, shards)))
    for k in range(1, grps):
        greet((lax.rem(g + k, grps), s))
    for d in loads[3:8]:
        d.start()

    def remote(src, dst, ssem, rsem, device):
        return pltpu.make_async_remote_copy(
            src_ref=src,
            dst_ref=dst,
            send_sem=ssem,
            recv_sem=rsem,
            device_id=device,
            device_id_type=MESH,
        )

    def plane(phase, k, src, dst):
        device = (g, lax.rem(s + k, shards))
        return remote(src, dst, plane_ssem.at[phase, k], plane_rsem.at[phase, k], device)

    def along(phase, k, src, dst):
        device = (lax.rem(g + k, grps), s)
        return remote(src, dst, z_ssem.at[phase, k], z_rsem.at[phase, k], device)

    def other(phase, src, dst):
        return remote(src, dst, core_ssem.at[phase], core_rsem.at[phase], (g, s + 1 - 2 * c))

    def place(phase, k, src, dst):
        device = (g, 2 * lax.rem(p + k, places) + c)
        return remote(src, dst, plane_ssem.at[phase, k], plane_rsem.at[phase, k], device)

    sends = []

    def start(copies):
        for d in copies:
            d.start()
        sends.extend(copies)
        return copies

    def z_spread(phase, buf):
        return start([along(phase, k, buf.at[g], buf.at[g]) for k in range(1, grps)])

    def recv(copies):
        for d in copies:
            d.wait_recv()

    def total(buf, n, *at):
        out = buf[(0,) + at].astype(F32)
        for i in range(1, n):
            out += buf[(i,) + at].astype(F32)
        return out

    for d in loads[:3]:
        d.wait()
    eye = square_eye(count)

    def route(touched_col, rows_ref, out, tag_out):
        n = touched_col.shape[0]
        cap = n // count * CAP
        hot = touched_col == iota((n, slots), 1)
        slot_col = jnp.sum(jnp.where(hot, block_slot[...].astype(F32), 0.0), axis=1, keepdims=True)
        slot_row = to_row(slot_col, square_eye(n))
        owner_col = jnp.floor((slot_col + 0.5) / local_blocks)
        owner_row = jnp.floor((slot_row + 0.5) / local_blocks)
        local_row = slot_row - owner_row * local_blocks
        at_col, at_row = iota((n, n), 0), iota((n, n), 1)
        line_col = jnp.floor((at_col + 0.5) / count)
        line_row = jnp.floor((at_row + 0.5) / count)
        earlier = (owner_col == owner_row) & (line_col == line_row) & (at_col < at_row)
        rank_row = jnp.sum(jnp.where(earlier, 1.0, 0.0), axis=0, keepdims=True)
        send_row = owner_row * cap + line_row[0:1, :] * CAP + rank_row
        picker = iota((shards * cap, n), 0) == send_row
        pick_f32 = jnp.where(picker, 1.0, 0.0)
        pick_bf = pick_f32.astype(BF16)
        filled = jnp.sum(pick_f32, axis=1, keepdims=True)
        local_col = jnp.sum(jnp.where(picker, local_row, 0.0), axis=1, keepdims=True)
        local_col = jnp.where(filled > 0.5, local_col, -1.0)
        for r in range(block_rows):
            part = rows_ref[pl.ds(r, n, stride=block_rows), :].astype(BF16)
            picked = mm(pick_bf, part).reshape(shards, cap, width)
            out[:, :, r * width : (r + 1) * width] = picked.astype(BF16)
        lanes = jnp.broadcast_to(local_col, (shards * cap, local_blocks))
        tag_out[...] = lanes.reshape(shards, cap, local_blocks).astype(BF16)

    def deliver(phase, send, land):
        land[s] = send[s]
        return start(
            [plane(phase, k, send.at[lax.rem(s + k, shards)], land.at[s]) for k in range(1, shards)]
        )

    rows_f32[...] = emb_grads[...].astype(F32)
    route(to_col(touched[...].astype(F32), eye), rows_f32, e_send, t_send)

    pl.semaphore_wait(barrier, shards + grps - 2)
    raw = start([along(2, k, emb_grads, raw_all.at[g]) for k in range(1, grps)])
    raw += start([along(1, k, touched, touched_all.at[g]) for k in range(1, grps)])
    near = deliver(3, e_send, e_recv) + deliver(2, t_send, t_recv)

    for d in loads[3:6]:
        d.wait()
    w1t[...] = o_w[0][...].T.astype(BF16)
    w2t[...] = o_w[1][...].T.astype(BF16)
    w2b[...] = o_w[1][...].astype(BF16)
    w3b[...] = o_w[2][...].astype(BF16)
    acc_one[...] = jnp.zeros_like(acc_one)
    acc_two[...] = jnp.zeros_like(acc_two)
    acc_three[...] = jnp.zeros_like(acc_three)

    for d in loads[6:8]:
        d.wait()
    for d in loads[8:]:
        d.start()

    def forward(i, carry):
        tok = pl.ds(pl.multiple_of(i * chunk, chunk), chunk)
        pre = mm(w1t[...], x[:, tok])
        logistic = 0.5 * jnp.tanh(0.5 * pre) + 0.5
        slope_buf[:, tok] = logistic
        hidden_one = (pre * logistic).astype(BF16)
        hidden_buf[:, tok] = hidden_one
        hid, slope = gate(mm(w2t[...], hidden_one))
        cc = cot[tok, :]
        acc_three[...] += mm(hid.astype(BF16), cc)
        back = (mm(w3b[...], cc, NT) * slope).astype(BF16)
        back_buf[:, tok] = back
        acc_two[...] += mm(hidden_one, back, NT)
        return carry

    back_chunk = min(1024, tokens)
    back_steps = tokens // back_chunk

    def backward(i, carry):
        tok = pl.ds(pl.multiple_of(i * back_chunk, back_chunk), back_chunk)
        logistic = slope_buf[:, tok]
        slope = logistic + hidden_buf[:, tok].astype(F32) * (1.0 - logistic)
        back = (mm(w2b[...], back_buf[:, tok]) * slope).astype(BF16)
        acc_one[0:din, :] += mm(x[:, tok], back, NT)
        return carry

    steps = tokens // chunk
    lax.fori_loop(0, steps, forward, 0)

    base = fold_two * h_two

    def folded(part):
        two = acc_two[pl.ds(pl.multiple_of(part * half_one, half_one), half_one), :]
        three = acc_three[pl.ds(pl.multiple_of(part * half_two, half_two), half_two), :]
        two = two.reshape(grps, fold_two * 8, h_two)
        three = three.reshape(grps, fold_three * 8, out_dim)
        out = [(a * h_two, two[:, 8 * a : 8 * a + 8, :]) for a in range(fold_two)]
        return out + [
            (base + b * out_dim, three[:, 8 * b : 8 * b + 8, :]) for b in range(fold_three)
        ]

    for at, piece in folded(1 - c):
        p_send[:, :, at : at + piece.shape[2]] = piece.astype(BF16)
    c_p = start([other(0, p_send, p_recv)])
    recv(raw)
    cols = []
    for k in range(1, grps):
        q = lax.rem(g + k, grps)
        raw_f32[pl.ds((k - 1) * count * block_rows, count * block_rows), :] = raw_all[q].astype(F32)
        cols.append(to_col(touched_all[q].astype(F32), eye))
    route(jnp.concatenate(cols, axis=0), raw_f32, f_send, u_send)
    far = deliver(6, f_send, f_recv) + deliver(7, u_send, u_recv)
    late = max(0, back_steps - TAIL)
    lax.fori_loop(0, late, backward, 0)
    recv(c_p)
    for at, piece in folded(c):
        there = p_recv[:, :, at : at + piece.shape[2]].astype(F32)
        q_send[:, :, at : at + piece.shape[2]] = (piece + there).astype(BF16)

    c_r = start(
        [along(3, k, q_send.at[lax.rem(g + k, grps)], r_recv.at[g]) for k in range(1, grps)]
    )
    r_recv[g] = q_send[g]

    lax.fori_loop(late, back_steps, backward, 0)
    thin = acc_one.shape[0] // 2
    my_rows = pl.ds(pl.multiple_of(c * thin, thin), thin)
    its_rows = pl.ds(pl.multiple_of((1 - c) * thin, thin), thin)
    c_s = start([other(1, acc_one.at[its_rows], s_recv)])

    for d in loads[8:]:
        d.wait()
    slot_eye = square_eye(local_blocks)
    table_col = to_col(slot_table[...].astype(F32), slot_eye)
    table_hot = table_col == iota((local_blocks, 128), 1)
    row_weight = jnp.zeros((local_blocks, width), F32)
    for r in range(block_rows):
        weight = o_table[pl.ds(r, local_blocks, stride=block_rows), :]
        row_weight += weight * weight
    weight_col = jnp.sum(row_weight, axis=1, keepdims=True)
    weight_row = jnp.sum(jnp.where(table_hot, weight_col, 0.0), axis=0, keepdims=True)

    recv(c_s)
    y_plane[p] = (acc_one[my_rows, :] + s_recv[...]).astype(BF16)
    c_yp = start([place(1, k, y_plane.at[p], y_plane.at[p]) for k in range(1, places)])
    recv(c_r)
    r_plane[p] = total(r_recv, grps).astype(BF16)
    c_rp = start([place(4, k, r_plane.at[p], r_plane.at[p]) for k in range(1, places)])

    recv(c_yp)
    y_z[g] = total(y_plane, places).astype(BF16)
    c_yz = z_spread(0, y_z)

    recv(c_rp)
    a_all[c, g] = total(r_plane, places).astype(BF16)
    c_ap = start([along(4, k, a_all.at[c, g], a_all.at[c, g]) for k in range(1, grps)])
    recv(near)
    recv(far)
    tags = jnp.concatenate(
        [
            t_recv[...].astype(F32).reshape(shards * CAP, local_blocks),
            u_recv[...].astype(F32).reshape(shards * (grps - 1) * CAP, local_blocks),
        ],
        axis=0,
    )
    match_f32 = jnp.where(tags == iota(tags.shape, 1), 1.0, 0.0)
    match_t = match_f32.T.astype(BF16)
    hits = to_col(jnp.sum(match_f32, axis=0, keepdims=True), slot_eye) > 0.5
    mask = jnp.broadcast_to(jnp.where(hits, 1.0, 0.0), (local_blocks, width)) > 0.5
    row_update = jnp.zeros((local_blocks, width), F32)
    for r in range(block_rows):
        at = pl.ds(r, local_blocks, stride=block_rows)
        lanes = slice(r * width, (r + 1) * width)
        rows_near = e_recv[:, :, lanes].astype(F32).reshape(shards * CAP, width)
        rows_far = f_recv[:, :, lanes].astype(F32).reshape(shards * (grps - 1) * CAP, width)
        summed = mm(match_t, jnp.concatenate([rows_near, rows_far], axis=0).astype(BF16))
        first_old, second_old = o_first[at, :], o_second[at, :]
        first, second, update = adam(first_old, second_old, summed, o_table[at, :])
        update = jnp.where(mask, update, 0.0)
        o_first[at, :] = jnp.where(mask, first, first_old)
        o_second[at, :] = jnp.where(mask, second, second_old)
        table_update[at, :] = update
        row_update += update * update
    update_col = jnp.sum(row_update, axis=1, keepdims=True)
    update_row = jnp.sum(jnp.where(table_hot, update_col, 0.0), axis=0, keepdims=True)
    stats[s] = jnp.concatenate([weight_row, update_row, jnp.zeros((6, 128), F32)], axis=0)
    c_st = start([plane(0, k, stats.at[s], stats.at[s]) for k in range(1, shards)])

    recv(c_yz)
    y_all[c] = total(y_z, grps)
    c_y = start([other(2, y_all.at[c], y_all.at[c])])
    weight_sq = [jnp.sum(w[...] * w[...], keepdims=True) for w in o_w]

    c_a = []
    for k in range(grps):
        i = lax.rem(g + grps - k, grps)
        if k:
            recv(c_ap[k - 1 : k])
        c_a += start([other(3 + k, a_all.at[c, i], a_all.at[c, i])])

    def dense_step(j, rows, grad, keep):
        first, second, update = adam(o_m[j][rows, :], o_v[j][rows, :], grad, o_w[j][rows, :])
        o_m[j][rows, :] = first
        o_v[j][rows, :] = second
        if keep is not None:
            keep[rows, :] = update
        return update, jnp.sum(update * update, axis=0, keepdims=True)

    def half_step(part):
        two = [
            a_all[part, :, :, a * h_two : (a + 1) * h_two].astype(F32) for a in range(fold_two)
        ]
        three = [
            a_all[part, :, :, base + b * out_dim : base + (b + 1) * out_dim].astype(F32)
            for b in range(fold_three)
        ]
        two = jnp.concatenate(two, axis=1).reshape(half_one, h_two)
        three = jnp.concatenate(three, axis=1).reshape(half_two, out_dim)
        rows_two = pl.ds(pl.multiple_of(part * half_one, half_one), half_one)
        rows_three = pl.ds(pl.multiple_of(part * half_two, half_two), half_two)
        return (
            dense_step(1, rows_two, two, update_two)[1],
            dense_step(2, rows_three, three, update_three)[1],
        )

    def trust(j, update_sq):
        return (
            learn_rate
            * jnp.sqrt(weight_sq[j])
            / (jnp.sqrt(jnp.sum(update_sq, keepdims=True)) + ratio_eps)
        )

    here = half_step(c)
    recv(c_y)
    grad = y_all[...].reshape(2 * thin, h_one)[0:din, :]
    update, update_sq = dense_step(0, slice(None), grad, None)
    o_w[0][...] = o_w[0][...] - trust(0, update_sq) * update

    recv(c_st)
    tot = total(stats, shards)
    ratio = jnp.sqrt(tot[0:1]) / (jnp.sqrt(tot[1:2]) + ratio_eps)
    ratio_col = jnp.sum(jnp.where(table_hot, ratio, 0.0), axis=1, keepdims=True)
    rate = jnp.broadcast_to(learn_rate * ratio_col, (local_blocks, width))
    for r in range(block_rows):
        at = pl.ds(r, local_blocks, stride=block_rows)
        o_table[at, :] = o_table[at, :] - rate * table_update[at, :]

    recv(c_a)
    there = half_step(1 - c)
    o_w[1][...] = o_w[1][...] - trust(1, here[0] + there[0]) * update_two[...]
    o_w[2][...] = o_w[2][...] - trust(2, here[1] + there[1]) * update_three[...]

    for d in sends:
        d.wait_send()


def store_kernel(*refs):
    srcs, outs, sem = refs[:12], refs[12:24], refs[24]
    stores = [pltpu.make_async_copy(a, b, sem.at[i]) for i, (a, b) in enumerate(zip(srcs, outs))]
    for d in stores:
        d.start()
    for d in stores:
        d.wait()


def body(
    table, table_first, table_second, slot_table, touched, emb_grads, block_slot,
    dense_x, dense_cot, *dense,
):
    shards = lax.axis_size("shard")
    grps = lax.axis_size("grp")
    blocks, block_rows, width = table.shape
    count = touched.shape[1]
    din, tokens = dense_x.shape
    h_one, h_two = dense[1].shape
    out_dim = dense[2].shape[1]
    chunk = min(1024, tokens)
    din_pad = -(-din // 16) * 16
    flat = (blocks * block_rows, width)
    e_width = block_rows * width
    places = shards // 2
    fold = (h_one // (16 * grps)) * h_two + (h_two // (16 * grps)) * out_dim
    hbm = pl.BlockSpec(memory_space=pltpu.HBM)
    vmem = pl.BlockSpec(memory_space=pltpu.VMEM)
    sds = jax.ShapeDtypeStruct
    state = tuple(a.reshape(flat) for a in (table, table_first, table_second)) + dense
    shapes = tuple(sds(a.shape, F32) for a in state)
    held = pl.pallas_call(
        functools.partial(exchange_kernel, grps, shards, chunk),
        out_shape=tuple(pltpu.VMEM(a.shape, F32) for a in state),
        in_specs=[hbm] * 18,
        out_specs=(vmem,) * 12,
        scratch_shapes=[
            pltpu.VMEM((1, count), jnp.int32),
            pltpu.VMEM((1, block_slot.shape[0]), jnp.int32),
            pltpu.VMEM((1, blocks), jnp.int32),
            pltpu.VMEM((count * block_rows, width), BF16),
            pltpu.VMEM(dense_x.shape, BF16),
            pltpu.VMEM(dense_cot.shape, BF16),
            pltpu.VMEM((h_one, din), BF16),
            pltpu.VMEM((h_two, h_one), BF16),
            pltpu.VMEM((h_one, h_two), BF16),
            pltpu.VMEM((h_two, out_dim), BF16),
            pltpu.VMEM((h_one, tokens), F32),
            pltpu.VMEM((h_one, tokens), BF16),
            pltpu.VMEM((h_two, tokens), BF16),
            pltpu.VMEM((din_pad, h_one), F32),
            pltpu.VMEM((h_one, h_two), F32),
            pltpu.VMEM((h_two, out_dim), F32),
            pltpu.VMEM((count * block_rows, width), F32),
            pltpu.VMEM((grps, count * block_rows, width), BF16),
            pltpu.VMEM(((grps - 1) * count * block_rows, width), F32),
            pltpu.VMEM((grps, 1, count), jnp.int32),
            pltpu.VMEM(flat, F32),
            pltpu.VMEM((h_one, h_two), F32),
            pltpu.VMEM((h_two, out_dim), F32),
            pltpu.VMEM((shards, CAP, e_width), BF16),
            pltpu.VMEM((shards, CAP, e_width), BF16),
            pltpu.VMEM((shards, CAP, blocks), BF16),
            pltpu.VMEM((shards, CAP, blocks), BF16),
            pltpu.VMEM((shards, (grps - 1) * CAP, e_width), BF16),
            pltpu.VMEM((shards, (grps - 1) * CAP, e_width), BF16),
            pltpu.VMEM((shards, (grps - 1) * CAP, blocks), BF16),
            pltpu.VMEM((shards, (grps - 1) * CAP, blocks), BF16),
            pltpu.VMEM((grps, 8, fold), BF16),
            pltpu.VMEM((grps, 8, fold), BF16),
            pltpu.VMEM((grps, 8, fold), BF16),
            pltpu.VMEM((grps, 8, fold), BF16),
            pltpu.VMEM((places, 8, fold), BF16),
            pltpu.VMEM((2, grps, 8, fold), BF16),
            pltpu.VMEM((din_pad // 2, h_one), F32),
            pltpu.VMEM((places, din_pad // 2, h_one), BF16),
            pltpu.VMEM((grps, din_pad // 2, h_one), BF16),
            pltpu.VMEM((2, din_pad // 2, h_one), F32),
            pltpu.VMEM((shards, 8, 128), F32),
            pltpu.SemaphoreType.DMA((8, shards)),
            pltpu.SemaphoreType.DMA((8, shards)),
            pltpu.SemaphoreType.DMA((5, grps)),
            pltpu.SemaphoreType.DMA((5, grps)),
            pltpu.SemaphoreType.DMA((3 + grps,)),
            pltpu.SemaphoreType.DMA((3 + grps,)),
            pltpu.SemaphoreType.DMA((18,)),
        ],
        compiler_params=pltpu.CompilerParams(
            collective_id=0, has_side_effects=True, vmem_limit_bytes=44 << 20
        ),
        name="tower_exchange",
    )(
        *(
            pltpu.with_memory_space_constraint(a, pltpu.HBM)
            for a in (
                touched,
                block_slot.reshape(1, -1),
                slot_table.reshape(1, -1),
                emb_grads.reshape(count * block_rows, width),
                dense_x,
                dense_cot,
            )
            + state
        )
    )
    outs = pl.pallas_call(
        store_kernel,
        out_shape=shapes,
        in_specs=[vmem] * 12,
        out_specs=(pl.BlockSpec(memory_space=pl.ANY),) * 12,
        scratch_shapes=[pltpu.SemaphoreType.DMA((12,))],
        compiler_params=pltpu.CompilerParams(vmem_limit_bytes=12 << 20),
        name="store",
    )(*held)
    return tuple(o.reshape(table.shape) for o in outs[:3]) + tuple(outs[3:])


def solution(mesh):
    dense = (P(),) * 9
    rows = P("shard", None, None)
    return jax.shard_map(
        body,
        mesh=mesh,
        in_specs=(
            rows,
            rows,
            rows,
            P("shard"),
            P("grp", "shard"),
            P("grp", "shard", None, None),
            P(),
            P(None, ("grp", "shard")),
            P(("grp", "shard"), None),
        )
        + dense,
        out_specs=(rows,) * 3 + dense,
        check_vma=False,
    )
```
